32 devices in a mesh: span: 8 (over z, x), plane: 4 (over y, core).
Axes of the slice: x: 2, y: 2, z: 4, core: 2. Of those that a mesh axis runs over, the one named last changes fastest.
Arguments:
- velocity: float32 [3, 1024, 512, 128], P(None, 'span', 'plane'), may hold values from -6 to 6
- wall_history: float32 [255, 1024, 512], P(None, 'span', 'plane'), may hold values from -6 to 6
- phase_bin: int32 [256], replicated, may hold values from 0 to 63
- station_of: int32 [1024], P('span'), may hold values from 0 to 31
- wall_index: int32 [512], P('plane'), may hold values from 0 to 7
Outputs:
- corrected: float32 [3, 1024, 512, 128], P(None, 'span', 'plane')
- pressure: float32 [1024, 512, 128], P('span', 'plane')
- coefficients: float32 [32, 8192], P('span')
The draws below stay inside these ranges and needn't reach their ends.
All inputs are finite; a program needn't handle non-finite values.
Results may differ from the reference program's by a relative error of at most 0.000078.
Values sent between devices are 32-bit elements; how exact they have to be, the bound alone decides.
No kernel may reach another device: no remote copies, remote signals or barrier semaphores. Data moves between devices by JAX's collectives and lax.ppermute only.
A program may use at most 192 MiB of HBM per device.

```python
import math
import jax
import jax.numpy as jnp
from jax import lax

NZ = 1024
NA = 128
NF = 64
NBIN = 64
ITERS = 4
WALL_SPAN = 8
RD = 128
HIST = 255
ST_DEV = 4
ZD = 128
NT = 512
NS = 256
NST = 32


def draw_station_of(key, part):
    keys = jax.random.split(jax.random.fold_in(key, 11), 2)
    owners = NZ // ZD
    plane_index = jnp.arange(NZ).astype(jnp.int32)
    home = plane_index // ZD
    local = plane_index % ZD
    spread = jax.random.randint(keys[0], (NZ,), 0, owners).astype(jnp.int32)
    target = jnp.where(local % 3 == 0, home - 1, jnp.where(local % 3 == 1, home + owners // 2, spread))
    target = (target + owners) % owners
    within = jax.random.randint(keys[1], (NZ,), 0, ST_DEV).astype(jnp.int32)
    return (target * ST_DEV + within).astype(jnp.int32)


def with_ends(entries, key, least, largest):
    longest = entries.shape.index(max(entries.shape))
    spots = []
    for shift in (0, 1):
        where = [jax.random.randint(jax.random.fold_in(key, axis), (), 0, length) for axis, length in enumerate(entries.shape)]
        where[longest] = (where[longest] + shift) % entries.shape[longest]
        spots.append(tuple(where))
    return entries.at[spots[0]].set(least).at[spots[1]].set(largest)


def steps_of(stream_key, dims, cuts, low, high):
    def one(axis_at, shards_of):
        draws = jax.random.uniform(jax.random.fold_in(jax.random.fold_in(stream_key, 6), axis_at), (shards_of,), jnp.float32, low / len(cuts), high / len(cuts))
        return jnp.repeat(jnp.exp(draws), dims[axis_at] // shards_of).reshape((-1,) + (1,) * (len(dims) - axis_at - 1))

    factor_of = one(*cuts[0])
    for cut in cuts[1:]:
        factor_of = factor_of * one(*cut)
    return factor_of


def noise(own_key, shape, scale, reach, cuts=(), kind=jnp.bfloat16):
    values = scale * jax.random.normal(own_key, shape, jnp.float32)
    if cuts:
        values = values * steps_of(own_key, shape, cuts, -0.22, 0.18)
    return jnp.clip(values, -reach, reach).astype(kind)


def setup_inputs(seed: int = 0) -> dict:
    key_of = jax.random.split(jax.random.key(seed), 6)
    return {
        "velocity": noise(key_of[0], (3, NZ, NT, RD), 1.0, 6.0, ((1, 8), (2, 4)), jnp.float32),
        "wall_history": noise(key_of[1], (HIST, NZ, NT), 1.0, 6.0, ((1, 8), (2, 4)), jnp.float32),
        "phase_bin": with_ends(jax.random.randint(key_of[2], (NS,), 0, NBIN), jax.random.fold_in(key_of[2], 1), 0, NBIN - 1).astype(jnp.int32),
        "station_of": draw_station_of(jax.random.fold_in(key_of[5], 71), 0),
        "wall_index": with_ends(jax.random.randint(key_of[4], (NT,), 0, WALL_SPAN), jax.random.fold_in(key_of[4], 1), 0, WALL_SPAN - 1).astype(jnp.int32),
    }


PRECISE = lax.Precision.HIGHEST

def hartley(field):
    spectrum = jnp.fft.fft(field, axis=0)
    return (jnp.real(spectrum) - jnp.imag(spectrum)).astype(field.dtype)

def radial_diff(field):
    padded = jnp.pad(field, ((0, 0), (0, 0), (1, 1)))
    return padded[..., 2:] - padded[..., :-2]

def radial_pair(field):
    padded = jnp.pad(field, ((0, 0), (0, 0), (1, 1)))
    return padded[..., :-2] + padded[..., 2:]

def mode_diagonal(modes):
    angle = 2.0 * math.pi / NZ * modes.astype(jnp.float32)
    return 6.0 - 2.0 * jnp.cos(angle)

def azimuth_basis(first_cell, cells, total):
    column = jnp.arange(NA).astype(jnp.int32)
    upper = column >= NA // 2
    harmonic = jnp.where(upper, column - NA // 2 + 1, column).astype(jnp.int32)
    index = (first_cell + jnp.arange(cells)).astype(jnp.int32)
    phase = index[:, None] * harmonic[None, :] % total
    angle = 2.0 * math.pi / total * phase.astype(jnp.float32)
    return jnp.where(upper[None, :], jnp.sin(angle), jnp.cos(angle))

def phase_weights(phase_bin, scale):
    column = jnp.arange(NF).astype(jnp.int32)
    upper = column >= NF // 2
    harmonic = jnp.where(upper, column - NF // 2 + 1, column).astype(jnp.int32)
    phase = phase_bin.astype(jnp.int32)[:, None] * harmonic[None, :] % NBIN
    angle = 2.0 * math.pi / NBIN * phase.astype(jnp.float32)
    return jnp.where(upper[None, :], jnp.sin(angle), jnp.cos(angle)) * scale

def reference(velocity, wall_history, phase_bin, station_of, wall_index):
    radial_v = velocity[0]
    azimuth_v = velocity[1]
    span_v = velocity[2]
    divergence = 0.5 * radial_diff(radial_v) + 0.5 * (jnp.roll(azimuth_v, -1, 1) - jnp.roll(azimuth_v, 1, 1)) + 0.5 * (jnp.roll(span_v, -1, 0) - jnp.roll(span_v, 1, 0))
    source = -divergence
    spectra = hartley(source)
    diagonal = mode_diagonal(jnp.arange(NZ))[:, None, None]
    potential = spectra / diagonal
    for sweep in range(ITERS):
        potential = (spectra + jnp.roll(potential, 1, 1) + jnp.roll(potential, -1, 1) + radial_pair(potential)) / diagonal
    pressure = hartley(potential) / NZ
    gradient = jnp.stack([0.5 * radial_diff(pressure), 0.5 * (jnp.roll(pressure, -1, 1) - jnp.roll(pressure, 1, 1)), 0.5 * (jnp.roll(pressure, -1, 0) - jnp.roll(pressure, 1, 0))])
    corrected = velocity - gradient
    wall_cells = jnp.broadcast_to(wall_index.astype(jnp.int32)[None, :, None], (NZ, NT, 1))
    wall_pressure = jnp.take_along_axis(pressure, wall_cells, axis=2)[..., 0]
    samples = jnp.concatenate([wall_history, wall_pressure[None]], axis=0)
    basis = azimuth_basis(0, NT, NT)
    amplitudes = jnp.dot(samples.reshape(NS * NZ, NT), basis, precision=PRECISE, preferred_element_type=jnp.float32).reshape(NS, NZ, NA)
    weights = phase_weights(phase_bin, 1.0 / math.sqrt(NT * NS))
    by_plane = jnp.einsum('tza,tf->zaf', amplitudes, weights, precision=PRECISE).reshape(NZ, NA * NF)
    selector = (station_of[:, None] == jnp.arange(NST)[None, :]).astype(jnp.float32)
    coefficients = jnp.dot(selector.T, by_plane, precision=PRECISE, preferred_element_type=jnp.float32)
    return (corrected, pressure, coefficients)
```

```python
import math

import jax
import jax.numpy as jnp
import numpy as np
from jax import lax
from jax.experimental import pallas as pl
from jax.experimental.pallas import tpu as pltpu
from jax.sharding import PartitionSpec as P

NZ = 1024
NA = 128
NF = 64
NBIN = 64
ITERS = 4
WALL_SPAN = 8
ST_DEV = 4
ORDER = ITERS + 1
TILE = 8
RHO = 3.0 - 2.0 * math.sqrt(2.0)
PRECISE = lax.Precision.HIGHEST


def representable(table):
    table = np.asarray(table, np.float64)
    return np.where(np.abs(table) < np.finfo(np.float32).tiny, 0.0, table).astype(np.float32)


def inverse_entry(distance):
    j = ORDER - 1
    return RHO ** (ORDER + distance) * sum(
        math.comb(j + i, j) * math.comb(j + distance + i, j) * RHO ** (2 * i) for i in range(40)
    )


def carry_weight(node, distance):
    basis = 1.0
    for other in range(ORDER):
        if other != node:
            basis *= (distance - other) / (node - other)
    return RHO ** (distance - node) * basis


def carry_table(cells):
    return representable([[carry_weight(b, d) for d in range(cells)] for b in range(ORDER)])


def hop_table(offset):
    return representable([[carry_weight(b, offset + d) for d in range(-1, ORDER)] for b in range(ORDER)])


def span_rows(cells):
    return cells + 3 * TILE


def solve_table(cells):
    rows = span_rows(cells)
    table = np.zeros((cells + TILE, rows))
    for i in range(cells + 2):
        for z in range(-ORDER - ITERS, cells + ORDER + ITERS):
            table[i, (z + TILE) % rows] = inverse_entry(abs(i - 1 - z))
    return representable(table)


def split(x):
    high = x.astype(jnp.bfloat16)
    low = (x - high.astype(jnp.float32)).astype(jnp.bfloat16)
    return high, low


def lane_pair(x, sign):
    axis = x.ndim - 1
    cells = x.shape[axis]
    lane = lax.broadcasted_iota(jnp.int32, x.shape, axis)
    low = jnp.where(lane == 0, 0.0, pltpu.roll(x, 1, axis))
    high = jnp.where(lane == cells - 1, 0.0, pltpu.roll(x, cells - 1, axis))
    return low + high if sign > 0 else low - high


def source_call(velocity):
    _, s_, t_, r_ = velocity.shape
    wide = t_ + 2 * TILE
    blocks = s_ // TILE
    table = carry_table(s_)
    reach = 1 + max(int(np.max(np.nonzero(row)[0])) for row in table) // TILE
    table = jnp.asarray(table)

    def kernel(tab, v, before, after, s_out, zr, zl, scr):
        c = pl.program_id(0)

        @pl.when(c == 0)
        def _():
            zr[...] = jnp.zeros_like(zr)
            zl[...] = jnp.zeros_like(zl)
            zl[ORDER, TILE : TILE + t_] = -0.5 * v[2, 0]

        @pl.when(c == blocks - 1)
        def _():
            zr[0, TILE : TILE + t_] = 0.5 * v[2, TILE - 1]

        @pl.when(c < blocks)
        def _():
            row = lax.broadcasted_iota(jnp.int32, (t_, r_), 0)
            tile_row = lax.broadcasted_iota(jnp.int32, (TILE, r_), 0)
            for i in range(TILE):
                if i == 0:
                    low = jnp.where(c == 0, 0.0, before[0, 0])
                else:
                    low = v[2, i - 1]
                if i == TILE - 1:
                    high = jnp.where(c == blocks - 1, 0.0, after[0, 0])
                else:
                    high = v[2, i + 1]
                turn = v[1, i]
                left = jnp.where(row == 0, 0.0, pltpu.roll(turn, 1, 0))
                right = jnp.where(row == t_ - 1, 0.0, pltpu.roll(turn, t_ - 1, 0))
                base = i * wide
                scr[base + TILE : base + TILE + t_] = 0.5 * (
                    lane_pair(v[0, i], -1) + (left - right) + (low - high)
                )
                first = pltpu.roll(turn[:TILE], TILE - 1, 0)
                last = pltpu.roll(turn[t_ - TILE :], 1, 0)
                scr[base : base + TILE] = jnp.where(tile_row == TILE - 1, -0.5 * first, 0.0)
                scr[base + TILE + t_ : base + wide] = jnp.where(tile_row == 0, 0.5 * last, 0.0)

            def move(t, _):
                s_out[t] = scr[pl.ds(t, TILE, stride=wide), :]
                return 0

            lax.fori_loop(0, wide, move, 0, unroll=8)

            def carry(out, first, flip):
                def tile(j, _):
                    at = pl.multiple_of(j * TILE, TILE)
                    cells = [scr[pl.ds(i * wide + at, TILE), :] for i in range(TILE)]
                    for b in range(ORDER):
                        total = out[first + (ORDER - 1 - b if flip else b), pl.ds(at, TILE), :]
                        for i in range(TILE):
                            z = c * TILE + i
                            total = total + tab[b, (s_ - 1 - z) if flip else z] * cells[i]
                        out[first + (ORDER - 1 - b if flip else b), pl.ds(at, TILE), :] = total
                    return 0

                lax.fori_loop(0, wide // TILE, tile, 0)

            @pl.when(c >= blocks - reach)
            def _():
                carry(zr, 1, True)

            @pl.when(c < reach)
            def _():
                carry(zl, 0, False)

        @pl.when(c == blocks)
        def _():
            s_out[...] = jnp.zeros_like(s_out)
            s_out[:, 0, :] = zr[0]
            s_out[:, TILE - 1, :] = zl[ORDER]

    return pl.pallas_call(
        kernel,
        grid=(blocks + 1,),
        in_specs=[
            pl.BlockSpec(memory_space=pltpu.SMEM),
            pl.BlockSpec((3, TILE, t_, r_), lambda c: (0, jnp.minimum(c, blocks - 1), 0, 0)),
            pl.BlockSpec((1, 1, t_, r_), lambda c: (2, jnp.clip(c * TILE - 1, 0, s_ - 1), 0, 0)),
            pl.BlockSpec((1, 1, t_, r_), lambda c: (2, jnp.minimum(c * TILE + TILE, s_ - 1), 0, 0)),
        ],
        out_specs=[
            pl.BlockSpec((wide, TILE, r_), lambda c: (0, c, 0)),
            pl.BlockSpec((ORDER + 1, wide, r_), lambda c: (0, 0, 0)),
            pl.BlockSpec((ORDER + 1, wide, r_), lambda c: (0, 0, 0)),
        ],
        out_shape=[
            jax.ShapeDtypeStruct((wide, s_ + TILE, r_), jnp.float32),
            jax.ShapeDtypeStruct((ORDER + 1, wide, r_), jnp.float32),
            jax.ShapeDtypeStruct((ORDER + 1, wide, r_), jnp.float32),
        ],
        scratch_shapes=[pltpu.VMEM((TILE * wide, r_), jnp.float32)],
        compiler_params=pltpu.CompilerParams(vmem_limit_bytes=40 << 20),
        name="source",
    )(table, velocity, velocity, velocity)


def bins_call(wall_history, phase_bin, station_of, basis, stations):
    h, s_, t_ = wall_history.shape
    step = max(d for d in range(1, 18) if h % d == 0)
    pair = 2
    def kernel(bins, x, station, base, out, acc):
        c = pl.program_id(0)

        @pl.when(c == 0)
        def _():
            acc[...] = jnp.zeros_like(acc)

        for i in range(step):
            b = bins[c * step + i]
            acc[b] += x[i]

        @pl.when(c == h // step - 1)
        def _():
            high, low = split(base[...])
            stack = jnp.concatenate([high, high, low], 0)
            pick = (lax.broadcasted_iota(jnp.int32, (stations, s_), 0) == station[...]).astype(jnp.bfloat16)

            def body(j, _):
                held = jnp.concatenate([acc[j * pair + q] for q in range(pair)], axis=1)
                top, rest = split(held)
                rows = jnp.dot(pick, top, preferred_element_type=jnp.float32) + jnp.dot(
                    pick, rest, preferred_element_type=jnp.float32
                )
                both = jnp.concatenate([rows[:, q * t_ : (q + 1) * t_] for q in range(pair)], axis=0)
                top, rest = split(both)
                tile = jnp.dot(
                    jnp.concatenate([top, rest, top], axis=1), stack, preferred_element_type=jnp.float32
                )
                for q in range(pair):
                    out[pl.ds(j * pair + q, stations, stride=NBIN), :] = tile[q * stations : (q + 1) * stations]
                return 0

            lax.fori_loop(0, NBIN // pair, body, 0, unroll=4)

    tiles = pl.pallas_call(
        kernel,
        grid_spec=pltpu.PrefetchScalarGridSpec(
            num_scalar_prefetch=1,
            grid=(h // step,),
            in_specs=[
                pl.BlockSpec((step, s_, t_), lambda c, bins: (c, 0, 0)),
                pl.BlockSpec((1, s_), lambda c, bins: (0, 0)),
                pl.BlockSpec((t_, NA), lambda c, bins: (0, 0)),
            ],
            out_specs=pl.BlockSpec((stations * NBIN, NA), lambda c, bins: (0, 0)),
            scratch_shapes=[pltpu.VMEM((NBIN, s_, t_), jnp.float32)],
        ),
        out_shape=jax.ShapeDtypeStruct((stations * NBIN, NA), jnp.float32),
        compiler_params=pltpu.CompilerParams(vmem_limit_bytes=40 << 20),
        name="bins",
    )(phase_bin, wall_history, station_of[None, :], basis)
    return tiles.reshape(stations, NBIN, NA)


def project_call(s_ext, pack_l, pack_r, velocity):
    _, s_, t_, r_ = velocity.shape
    wide = t_ + 2 * TILE
    rows = span_rows(s_)
    held = rows + (-rows) % (2 * TILE)
    out_rows = s_ + TILE
    steps = wide // TILE
    lag = TILE + ITERS
    table = np.pad(solve_table(s_), ((0, 0), (0, held - rows)))
    top = table.astype(jnp.bfloat16)
    rest = (table - top.astype(np.float32)).astype(jnp.bfloat16)
    table = jnp.asarray(np.concatenate([top, rest], 0))
    slots = TILE + 2

    def kernel(s_in, near, far, v, tab, corrected, pressure, a0, a1, a2, a3, w1, w2, w3, high, low, pot, pn, gn):
        k = pl.program_id(0)
        levels_a = [a0, a1, a2, a3]
        levels_w = [a0, w1, w2, w3]
        row = lax.broadcasted_iota(jnp.int32, (TILE, r_), 0)

        @pl.when(k == 0)
        def _():
            for ref in (a0, a1, a2, a3, w1, w2, w3):
                ref[TILE:slots] = jnp.zeros((2, rows, r_), jnp.float32)
            pot[TILE:] = jnp.zeros((TILE, out_rows, r_), jnp.float32)

        for ref in (a0, a1, a2, a3, w1, w2, w3):
            ref[0:2] = ref[TILE:slots]
        pot[:TILE] = pot[TILE:]

        def load(i, _):
            t = k * TILE + i
            own = s_in[i]
            edge = own[s_:]
            low_tile = near[pl.ds(t, TILE, stride=wide), :]
            high_tile = far[pl.ds(t, TILE, stride=wide), :]
            a0[i + 2, 0:TILE] = jnp.where(row >= TILE - ORDER, low_tile, 0.0) + jnp.where(row == TILE - 1, edge, 0.0)
            a0[i + 2, TILE : TILE + s_] = own[:s_]
            a0[i + 2, TILE : 2 * TILE] += jnp.where(row == 0, low_tile, 0.0)
            a0[i + 2, s_ : s_ + TILE] += jnp.where(row == TILE - 1, high_tile, 0.0)
            a0[i + 2, s_ + TILE : s_ + 2 * TILE] = jnp.where(row < ORDER, high_tile, 0.0) + jnp.where(row == 0, edge, 0.0)
            a0[i + 2, s_ + 2 * TILE :] = jnp.zeros((TILE, r_), jnp.float32)
            return 0

        lax.fori_loop(0, TILE, load, 0)

        for n in range(1, ITERS + 1):
            past, weighted = levels_a[n - 1], levels_w[n - 1]

            def sweep(i, _, n=n, past=past, weighted=weighted):
                total = past[i] + past[i + 2] + lane_pair(past[i + 1], 1)
                mid = weighted[i + 1]
                value = 6.0 * mid - (pltpu.roll(mid, 1, 0) + pltpu.roll(mid, rows - 1, 0)) + total
                if n < ITERS:
                    levels_a[n][i + 2] = total
                    levels_w[n][i + 2] = value
                else:
                    value = jnp.concatenate([value, jnp.zeros((held - rows, r_), jnp.float32)], 0)
                    top_part, rest_part = split(value)
                    at = pl.multiple_of(i * r_, r_)
                    high[:, pl.ds(at, r_)] = top_part
                    low[:, pl.ds(at, r_)] = rest_part
                return 0

            lax.fori_loop(0, TILE, sweep, 0)

        one = jnp.dot(tab[...], high[...], preferred_element_type=jnp.float32)
        two = jnp.dot(tab[:out_rows], low[...], preferred_element_type=jnp.float32)
        total = one[:out_rows] + one[out_rows:] + two
        for i in range(TILE):
            pot[TILE + i] = total[:, i * r_ : (i + 1) * r_]

        @pl.when(k >= 2)
        def _():
            for i in range(TILE):
                at = ITERS + i
                pn[pl.ds(i, out_rows, stride=TILE), :] = pot[at]
                gn[pl.ds(i, out_rows, stride=TILE), :] = pot[at + 1] - pot[at - 1]

            def finish(z, _):
                mid = pn[pl.ds(pl.multiple_of((z + 1) * TILE, TILE), TILE), :]
                down = pn[pl.ds(pl.multiple_of(z * TILE, TILE), TILE), :]
                up = pn[pl.ds(pl.multiple_of((z + 2) * TILE, TILE), TILE), :]
                turn = gn[pl.ds(pl.multiple_of((z + 1) * TILE, TILE), TILE), :]
                pressure[z] = mid
                corrected[0, z] = v[0, z] + 0.5 * lane_pair(mid, -1)
                corrected[1, z] = v[1, z] - 0.5 * turn
                corrected[2, z] = v[2, z] - 0.5 * (up - down)
                return 0

            lax.fori_loop(0, s_, finish, 0, unroll=8)

    at = lambda k: jnp.maximum(k - 2, 0)
    slab = pltpu.VMEM((slots, rows, r_), jnp.float32)
    return pl.pallas_call(
        kernel,
        grid=(steps,),
        in_specs=[
            pl.BlockSpec((TILE, s_ + TILE, r_), lambda k: (k, 0, 0)),
            pl.BlockSpec((TILE * wide, r_), lambda k: (0, 0)),
            pl.BlockSpec((TILE * wide, r_), lambda k: (0, 0)),
            pl.BlockSpec((3, s_, TILE, r_), lambda k: (0, 0, at(k), 0)),
            pl.BlockSpec((2 * out_rows, held), lambda k: (0, 0)),
        ],
        out_specs=[
            pl.BlockSpec((3, s_, TILE, r_), lambda k: (0, 0, at(k), 0)),
            pl.BlockSpec((s_, TILE, r_), lambda k: (0, at(k), 0)),
        ],
        out_shape=[
            jax.ShapeDtypeStruct(velocity.shape, jnp.float32),
            jax.ShapeDtypeStruct(velocity.shape[1:], jnp.float32),
        ],
        scratch_shapes=[slab] * 7
        + [
            pltpu.VMEM((held, TILE * r_), jnp.bfloat16),
            pltpu.VMEM((held, TILE * r_), jnp.bfloat16),
            pltpu.VMEM((2 * TILE, out_rows, r_), jnp.float32),
            pltpu.VMEM((out_rows * TILE, r_), jnp.float32),
            pltpu.VMEM((out_rows * TILE, r_), jnp.float32),
        ],
        compiler_params=pltpu.CompilerParams(vmem_limit_bytes=56 << 20),
        name="project",
    )(s_ext, pack_l.reshape(TILE * wide, r_), pack_r.reshape(TILE * wide, r_), velocity, table)


def azimuth_basis(first_cell, cells, total):
    column = jnp.arange(NA)
    upper = column >= NA // 2
    harmonic = jnp.where(upper, column - NA // 2 + 1, column)
    index = first_cell + jnp.arange(cells)
    phase = index[:, None] * harmonic[None, :] % total
    angle = 2.0 * math.pi / total * phase.astype(jnp.float32)
    return jnp.where(upper[None, :], jnp.sin(angle), jnp.cos(angle))


def bin_weights(scale):
    column = jnp.arange(NF)
    upper = column >= NF // 2
    harmonic = jnp.where(upper, column - NF // 2 + 1, column)
    phase = jnp.arange(NBIN)[:, None] * harmonic[None, :] % NBIN
    angle = 2.0 * math.pi / NBIN * phase.astype(jnp.float32)
    return jnp.where(upper[None, :], jnp.sin(angle), jnp.cos(angle)) * scale


def send(x, spans, planes, by_span, by_plane):
    pairs = []
    for i in range(spans):
        for j in range(planes):
            to = ((i + by_span) % spans) * planes + (j + by_plane) % planes
            pairs.append((i * planes + j, to))
    return lax.ppermute(x, ("span", "plane"), pairs)


def exchange(s_ext, zr, zl, spans, planes, span_cells, theta_cells):
    edge = ORDER + 1
    first = TILE - 1
    last = TILE + theta_cells - ORDER
    after = TILE - ORDER
    before = TILE + theta_cells - 1

    def widen(low, mid, high):
        total = mid.shape[1]
        low = jnp.pad(low, ((0, 0), (after, total - after - edge), (0, 0)))
        high = jnp.pad(high, ((0, 0), (before, total - before - edge), (0, 0)))
        return mid + low + high

    def planes_of(z, step):
        mid = send(z, spans, planes, step, 0)
        low = send(z[:, last : last + edge], spans, planes, step, 1)
        high = send(z[:, first : first + edge], spans, planes, step, -1)
        return widen(low, mid, high)

    low = send(s_ext[last : last + edge], spans, planes, 0, 1)
    high = send(s_ext[first : first + edge], spans, planes, 0, -1)
    from_left = planes_of(zr, 1)
    from_right = planes_of(zl, -1)
    hop = 1
    while hop < spans and np.any(hop_table(hop * span_cells)):
        table = hop_table(hop * span_cells)
        far_left = planes_of(zr, hop + 1)
        far_right = planes_of(zl, -hop - 1)
        from_left = from_left.at[1:].add(
            jnp.einsum("bd,dar->bar", table[::-1], jnp.concatenate([far_left[:1], far_left[:0:-1]], 0), precision=PRECISE))
        from_right = from_right.at[:-1].add(
            jnp.einsum("bd,dar->bar", table, jnp.concatenate([far_right[-1:], far_right[:-1]], 0), precision=PRECISE))
        hop += 1
    s_ext = s_ext.at[after : after + edge].add(low).at[before : before + edge].add(high)
    gap = jnp.zeros((2,) + zr.shape[1:], zr.dtype)
    pack_l = jnp.concatenate([from_left[:1], gap, from_left[1:]], 0)
    pack_r = jnp.concatenate([from_right[:-1], gap, from_right[-1:]], 0)
    return s_ext, pack_l, pack_r


def local(velocity, wall_history, phase_bin, station_of, wall_index, spans, planes):
    _, span_cells, theta_cells, _ = velocity.shape
    total_theta = theta_cells * planes
    stations = ST_DEV * spans
    basis = azimuth_basis(lax.axis_index("plane") * theta_cells, theta_cells, total_theta)
    s_ext, zr, zl = source_call(velocity)
    tiles = bins_call(wall_history, phase_bin, station_of, basis, stations)
    s_ext, pack_l, pack_r = exchange(s_ext, zr, zl, spans, planes, span_cells, theta_cells)
    held = lax.psum_scatter(tiles, "span", scatter_dimension=0, tiled=True)
    held = lax.psum(held, "plane")
    corrected, pressure = project_call(s_ext, pack_l, pack_r, velocity)
    wall_select = (wall_index[:, None] == jnp.arange(WALL_SPAN)[None, :]).astype(jnp.float32)
    wall = jnp.sum(pressure[:, :, :WALL_SPAN] * wall_select[None, :, :], axis=2)
    selector = (station_of[:, None] == jnp.arange(stations)[None, :]).astype(jnp.float32)
    wall_tile = jnp.dot(jnp.dot(selector.T, wall, precision=PRECISE), basis, precision=PRECISE)
    wall_tile = lax.psum(lax.psum_scatter(wall_tile, "span", scatter_dimension=0, tiled=True), "plane")
    newest = (jnp.arange(NBIN) == phase_bin[-1]).astype(jnp.float32)
    held = held + newest[None, :, None] * wall_tile[:, None, :]
    weights = bin_weights(1.0 / math.sqrt(total_theta * (wall_history.shape[0] + 1)))
    coefficients = jnp.einsum("sba,bf->saf", held, weights, precision=PRECISE).reshape(ST_DEV, NA * NF)
    return corrected, pressure, coefficients


def solution(mesh):
    spans = mesh.shape["span"]
    planes = mesh.shape["plane"]
    in_specs = (
        P(None, "span", "plane", None),
        P(None, "span", "plane"),
        P(),
        P("span"),
        P("plane"),
    )
    out_specs = (P(None, "span", "plane", None), P("span", "plane", None), P("span", None))

    def body(*args):
        return local(*args, spans, planes)

    return jax.shard_map(body, mesh=mesh, in_specs=in_specs, out_specs=out_specs, check_vma=False)
```

```python
import math

import jax
import jax.numpy as jnp
import numpy as np
from jax import lax
from jax.experimental import pallas as pl
from jax.experimental.pallas import tpu as pltpu
from jax.sharding import PartitionSpec as P

NZ = 1024
NA = 128
NF = 64
NBIN = 64
ITERS = 4
WALL_SPAN = 8
ST_DEV = 4
ORDER = ITERS + 1
TILE = 8
LEAD = 9
RHO = 3.0 - 2.0 * math.sqrt(2.0)
PRECISE = lax.Precision.HIGHEST


def representable(table):
    table = np.asarray(table, np.float64)
    return np.where(np.abs(table) < np.finfo(np.float32).tiny, 0.0, table).astype(np.float32)


def inverse_entry(distance, order=ORDER):
    j = order - 1
    return RHO ** (order + distance) * sum(
        math.comb(j + i, j) * math.comb(j + distance + i, j) * RHO ** (2 * i) for i in range(40)
    )


def carry_weight(node, distance):
    basis = 1.0
    for other in range(ORDER):
        if other != node:
            basis *= (distance - other) / (node - other)
    return RHO ** (distance - node) * basis


def carry_table(cells):
    return representable([[carry_weight(b, d) for d in range(cells)] for b in range(ORDER)])


def hop_table(offset):
    return representable([[carry_weight(b, offset + d) for d in range(-1, ORDER)] for b in range(ORDER)])


def radial_modes(cells):
    index = np.arange(1, cells + 1)
    return math.sqrt(2.0 / (cells + 1)) * np.sin(np.pi * np.outer(index, index) / (cells + 1))


def radial_rates(cells):
    return (2.0 * np.cos(np.pi * np.arange(1, cells + 1) / (cells + 1))).astype(np.float32)


def radial_step(cells):
    return 0.5 * (np.eye(cells, k=-1) - np.eye(cells, k=1))


def stacked(table):
    table = np.asarray(table, np.float32)
    top = table.astype(jnp.bfloat16)
    rest = (table - top.astype(np.float32)).astype(jnp.bfloat16)
    return np.concatenate([top, top, rest], 0)


def span_rows(cells):
    return cells + 3 * TILE


def solve_table(cells):
    rows = span_rows(cells)
    table = np.zeros((cells + TILE, rows))
    entries = [inverse_entry(d) for d in range(cells + 2 * TILE)]
    for i in range(cells + 2):
        for z in range(-ORDER - ITERS, cells + ORDER + ITERS):
            table[i, (z + TILE) % rows] = entries[abs(i - 1 - z)]
    return representable(table)


def wall_table(cells):
    table = np.zeros((ORDER, cells, cells + 2 * TILE))
    for j in range(ORDER):
        entries = [inverse_entry(d, j + 1) for d in range(cells + ORDER)]
        for i in range(cells):
            for z in range(-ORDER, cells + ORDER):
                table[j, i, z + TILE] = entries[abs(i - z)]
    return representable(table)


def split(x):
    high = x.astype(jnp.bfloat16)
    low = (x - high.astype(jnp.float32)).astype(jnp.bfloat16)
    return high, low


def triple(x):
    high, low = split(x)
    return jnp.concatenate([high, low, high], axis=1)


def source_call(velocity):
    _, s_, t_, r_ = velocity.shape
    wide = t_ + 2 * TILE
    blocks = t_ // TILE
    tall = s_ + TILE
    modes = radial_modes(r_)
    both = jnp.asarray(np.concatenate([stacked(-radial_step(r_) @ modes), stacked(modes)], 0))
    carry = carry_table(s_)
    table = np.zeros((2 * TILE, s_), np.float32)
    for b in range(ORDER):
        table[TILE - 1 - b] = carry[b, ::-1]
        table[TILE + b] = carry[b]
    top = table.astype(jnp.bfloat16)
    rest = (table - top.astype(np.float32)).astype(jnp.bfloat16)
    table = jnp.asarray(np.concatenate([top, rest], 0))

    def kernel(radial, turn, along, tab, both_ref, s_out, zr, zl, keep, hold, lhs, high, low):
        k = pl.program_id(0)

        @pl.when(k == 0)
        def _():
            keep[...] = jnp.zeros_like(keep)
            hold[...] = jnp.zeros_like(hold)
            s_out[...] = jnp.zeros_like(s_out)
            zr[...] = jnp.zeros_like(zr)
            zl[...] = jnp.zeros_like(zl)

        @pl.when(k > 0)
        def _():
            inside = k <= blocks
            pad = jnp.zeros((TILE, r_), jnp.float32)
            for i in range(TILE):
                at = pl.ds(i, s_, stride=TILE)
                x0, x1, x2 = radial[at, :], turn[at, :], along[at, :]
                x0 = jnp.where(inside, x0, 0.0)
                x1 = jnp.where(inside, x1, 0.0)
                x2 = jnp.concatenate([jnp.where(inside, x2, 0.0), pad], 0)
                across = jnp.concatenate([0.5 * (keep[0] - x1), pad], 0)
                lhs[i * tall : (i + 1) * tall, 3 * r_ :] = triple(hold[...] + across)
                hold[...] = 0.5 * (pltpu.roll(x2, 1, 0) - pltpu.roll(x2, tall - 1, 0))
                keep[0] = keep[1]
                keep[1] = x1
                lhs[i * tall : (i + 1) * tall, : 3 * r_] = triple(jnp.concatenate([keep[2], pad], 0))
                keep[2] = x0
            value = jnp.dot(lhs[...], both_ref[...], preferred_element_type=jnp.float32)
            for i in range(TILE):
                own = value[i * tall : (i + 1) * tall]
                s_out[i] = own
                top, rest = split(own[:s_])
                high[:, i * r_ : (i + 1) * r_] = top
                low[:, i * r_ : (i + 1) * r_] = rest
            one = jnp.dot(tab[...], high[...], preferred_element_type=jnp.float32)
            two = jnp.dot(tab[: 2 * TILE], low[...], preferred_element_type=jnp.float32)
            planes = one[: 2 * TILE] + one[2 * TILE :] + two
            row = lax.broadcasted_iota(jnp.int32, (TILE, r_), 0)
            for i in range(TILE):
                edge = s_out[i, s_:]
                here = planes[:, i * r_ : (i + 1) * r_]
                zr[i] = here[:TILE] + jnp.where(row == 0, edge, 0.0)
                zl[i] = here[TILE:] + jnp.where(row == TILE - 1, edge, 0.0)

    def part(axis):
        return pl.BlockSpec((1, s_, TILE, r_), lambda k: (axis, 0, jnp.clip(k - 1, 0, blocks - 1), 0))

    def flat(ref):
        return ref.reshape(s_ * TILE, r_)

    def body(x0, x1, x2, *refs):
        kernel(flat(x0.at[0]), flat(x1.at[0]), flat(x2.at[0]), *refs)

    return pl.pallas_call(
        body,
        grid=(wide // TILE,),
        in_specs=[
            part(0),
            part(1),
            part(2),
            pl.BlockSpec((4 * TILE, s_), lambda k: (0, 0)),
            pl.BlockSpec((6 * r_, r_), lambda k: (0, 0)),
        ],
        out_specs=[
            pl.BlockSpec((TILE, tall, r_), lambda k: (k, 0, 0)),
            pl.BlockSpec((TILE, TILE, r_), lambda k: (k, 0, 0)),
            pl.BlockSpec((TILE, TILE, r_), lambda k: (k, 0, 0)),
        ],
        out_shape=[
            jax.ShapeDtypeStruct((wide, tall, r_), jnp.float32),
            jax.ShapeDtypeStruct((wide, TILE, r_), jnp.float32),
            jax.ShapeDtypeStruct((wide, TILE, r_), jnp.float32),
        ],
        scratch_shapes=[
            pltpu.VMEM((3, s_, r_), jnp.float32),
            pltpu.VMEM((tall, r_), jnp.float32),
            pltpu.VMEM((TILE * tall, 6 * r_), jnp.bfloat16),
            pltpu.VMEM((s_, TILE * r_), jnp.bfloat16),
            pltpu.VMEM((s_, TILE * r_), jnp.bfloat16),
        ],
        compiler_params=pltpu.CompilerParams(vmem_limit_bytes=40 << 20),
        name="source",
    )(velocity, velocity, velocity, table, both)


def bins_call(wall_history, phase_bin, station_of, basis, stations):
    h, s_, t_ = wall_history.shape
    step = max(d for d in range(1, 52) if h % d == 0)
    pair = 2
    def kernel(bins, x, station, base, out, acc):
        c = pl.program_id(0)

        @pl.when(c == 0)
        def _():
            acc[...] = jnp.zeros_like(acc)

        for i in range(step):
            b = bins[c * step + i]
            acc[b] += x[i]

        @pl.when(c == h // step - 1)
        def _():
            high, low = split(base[...])
            stack = jnp.concatenate([high, high, low], 0)
            pick = (lax.broadcasted_iota(jnp.int32, (stations, s_), 0) == station[...]).astype(jnp.bfloat16)

            def body(j, _):
                held = jnp.concatenate([acc[j * pair + q] for q in range(pair)], axis=1)
                top, rest = split(held)
                rows = jnp.dot(pick, top, preferred_element_type=jnp.float32) + jnp.dot(
                    pick, rest, preferred_element_type=jnp.float32
                )
                both = jnp.concatenate([rows[:, q * t_ : (q + 1) * t_] for q in range(pair)], axis=0)
                top, rest = split(both)
                tile = jnp.dot(
                    jnp.concatenate([top, rest, top], axis=1), stack, preferred_element_type=jnp.float32
                )
                for q in range(pair):
                    out[pl.ds(j * pair + q, stations, stride=NBIN), :] = tile[q * stations : (q + 1) * stations]
                return 0

            lax.fori_loop(0, NBIN // pair, body, 0, unroll=4)

    tiles = pl.pallas_call(
        kernel,
        grid_spec=pltpu.PrefetchScalarGridSpec(
            num_scalar_prefetch=1,
            grid=(h // step,),
            in_specs=[
                pl.BlockSpec((step, s_, t_), lambda c, bins: (c, 0, 0)),
                pl.BlockSpec((1, s_), lambda c, bins: (0, 0)),
                pl.BlockSpec((t_, NA), lambda c, bins: (0, 0)),
            ],
            out_specs=pl.BlockSpec((stations * NBIN, NA), lambda c, bins: (0, 0)),
            scratch_shapes=[pltpu.VMEM((NBIN, s_, t_), jnp.float32)],
        ),
        out_shape=jax.ShapeDtypeStruct((stations * NBIN, NA), jnp.float32),
        compiler_params=pltpu.CompilerParams(vmem_limit_bytes=40 << 20),
        name="bins",
    )(phase_bin, wall_history, station_of[None, :], basis)
    return tiles.reshape(stations, NBIN, NA)


def slab_parts(own, low, high, cells):
    row = lax.broadcasted_iota(jnp.int32, (TILE, own.shape[-1]), 0)
    edge = own[cells:]
    before = jnp.where(row >= TILE - ORDER, low, 0.0) + jnp.where(row == TILE - 1, edge, 0.0)
    after = jnp.where(row < ORDER, high, 0.0) + jnp.where(row == 0, edge, 0.0)
    return before, jnp.where(row == 0, low, 0.0), jnp.where(row == TILE - 1, high, 0.0), after


def project_call(s_ext, pack_l, pack_r, velocity):
    _, s_, t_, r_ = velocity.shape
    wide = t_ + 2 * TILE
    rows = span_rows(s_)
    held = rows + (-rows) % (2 * TILE)
    out_rows = s_ + TILE
    steps = wide // TILE
    table = np.pad(solve_table(s_), ((0, 0), (0, held - rows)))
    top = table.astype(jnp.bfloat16)
    rest = (table - top.astype(np.float32)).astype(jnp.bfloat16)
    table = jnp.asarray(np.concatenate([top, rest], 0))
    modes = radial_modes(r_)
    back = jnp.asarray(np.concatenate([stacked(modes), stacked(modes @ radial_step(r_))], 1))
    rates = jnp.asarray(radial_rates(r_))[None, :]
    slots = TILE + 2

    def kernel(s_in, near, far, v, tab, turn, rate, corrected, pressure, *scratch):
        a0, a1, a2, a3, w1, w2, w3, high, low, pot, rad, pn, gn, rn = scratch
        k = pl.program_id(0)
        levels_a = [a0, a1, a2, a3]
        levels_w = [a0, w1, w2, w3]

        @pl.when(k == 0)
        def _():
            for ref in (a0, a1, a2, a3, w1, w2, w3):
                ref[TILE:slots] = jnp.zeros((2, rows, r_), jnp.float32)
            a0[:, rows - TILE :] = jnp.zeros((slots, TILE, r_), jnp.float32)
            pot[TILE:] = jnp.zeros((TILE, out_rows, r_), jnp.float32)
            rad[TILE:] = jnp.zeros((TILE, out_rows, r_), jnp.float32)

        for ref in (a0, a1, a2, a3, w1, w2, w3):
            ref[0:2] = ref[TILE:slots]
        pot[:TILE] = pot[TILE:]
        rad[:TILE] = rad[TILE:]

        def load(i, _):
            own = s_in[i]
            before, at_low, at_high, after = slab_parts(own, near[i], far[i], s_)
            a0[i + 2, 0:TILE] = before
            a0[i + 2, TILE : TILE + s_] = own[:s_]
            a0[i + 2, TILE : 2 * TILE] += at_low
            a0[i + 2, s_ : s_ + TILE] += at_high
            a0[i + 2, s_ + TILE : s_ + 2 * TILE] = after
            return 0

        lax.fori_loop(0, TILE, load, 0)

        for n in range(1, ITERS + 1):
            past, weighted = levels_a[n - 1], levels_w[n - 1]

            def sweep(i, _, n=n, past=past, weighted=weighted):
                total = past[i] + past[i + 2] + rate[...] * past[i + 1]
                mid = weighted[i + 1]
                value = 6.0 * mid - (pltpu.roll(mid, 1, 0) + pltpu.roll(mid, rows - 1, 0)) + total
                if n < ITERS:
                    levels_a[n][i + 2] = total
                    levels_w[n][i + 2] = value
                else:
                    value = jnp.concatenate([value, jnp.zeros((held - rows, r_), jnp.float32)], 0)
                    top_part, rest_part = split(value)
                    at = pl.multiple_of(i * r_, r_)
                    high[:, pl.ds(at, r_)] = top_part
                    low[:, pl.ds(at, r_)] = rest_part
                return 0

            lax.fori_loop(0, TILE, sweep, 0)

        one = jnp.dot(tab[...], high[...], preferred_element_type=jnp.float32)
        two = jnp.dot(tab[:out_rows], low[...], preferred_element_type=jnp.float32)
        total = one[:out_rows] + one[out_rows:] + two
        for i in range(TILE):
            here = jnp.dot(triple(total[:, i * r_ : (i + 1) * r_]), turn[...], preferred_element_type=jnp.float32)
            pot[TILE + i] = here[:, :r_]
            rad[TILE + i] = here[:, r_:]

        @pl.when(k >= 2)
        def _():
            for i in range(TILE):
                at = LEAD - ORDER + 1 + i
                pn[pl.ds(i, out_rows, stride=TILE), :] = pot[at]
                rn[pl.ds(i, out_rows, stride=TILE), :] = rad[at]
                gn[pl.ds(i, out_rows, stride=TILE), :] = 0.5 * (pot[at + 1] - pot[at - 1])

            def finish(z, _):
                here = pl.ds(pl.multiple_of((z + 1) * TILE, TILE), TILE)
                down = pn[pl.ds(pl.multiple_of(z * TILE, TILE), TILE), :]
                up = pn[pl.ds(pl.multiple_of((z + 2) * TILE, TILE), TILE), :]
                pressure[z] = pn[here, :]
                corrected[0, z] = v[0, z] - rn[here, :]
                corrected[1, z] = v[1, z] - gn[here, :]
                corrected[2, z] = v[2, z] - 0.5 * (up - down)
                return 0

            lax.fori_loop(0, s_, finish, 0, unroll=8)

    at = lambda k: jnp.maximum(k - 2, 0)
    slab = pltpu.VMEM((slots, rows, r_), jnp.float32)
    return pl.pallas_call(
        kernel,
        grid=(steps,),
        in_specs=[
            pl.BlockSpec((TILE, s_ + TILE, r_), lambda k: (k, 0, 0)),
            pl.BlockSpec((TILE, TILE, r_), lambda k: (k, 0, 0)),
            pl.BlockSpec((TILE, TILE, r_), lambda k: (k, 0, 0)),
            pl.BlockSpec((3, s_, TILE, r_), lambda k: (0, 0, at(k), 0)),
            pl.BlockSpec((2 * out_rows, held), lambda k: (0, 0)),
            pl.BlockSpec((3 * r_, 2 * r_), lambda k: (0, 0)),
            pl.BlockSpec((1, r_), lambda k: (0, 0)),
        ],
        out_specs=[
            pl.BlockSpec((3, s_, TILE, r_), lambda k: (0, 0, at(k), 0)),
            pl.BlockSpec((s_, TILE, r_), lambda k: (0, at(k), 0)),
        ],
        out_shape=[
            jax.ShapeDtypeStruct(velocity.shape, jnp.float32),
            jax.ShapeDtypeStruct(velocity.shape[1:], jnp.float32),
        ],
        scratch_shapes=[slab] * 7
        + [pltpu.VMEM((held, TILE * r_), jnp.bfloat16)] * 2
        + [pltpu.VMEM((2 * TILE, out_rows, r_), jnp.float32)] * 2
        + [pltpu.VMEM((out_rows * TILE, r_), jnp.float32)] * 3,
        compiler_params=pltpu.CompilerParams(vmem_limit_bytes=56 << 20),
        name="project",
    )(s_ext, pack_l, pack_r, velocity, table, back, rates)


def wall_call(s_ext, pack_l, pack_r, station_of, wall_index, basis, stations):
    wide, tall, r_ = s_ext.shape
    s_ = tall - TILE
    t_ = wide - 2 * TILE
    rows = s_ + 2 * TILE
    steps = wide // TILE
    pitch = rows + (-rows) % r_
    table = np.pad(wall_table(s_), ((0, 0), (0, 0), (0, pitch - rows))).transpose(1, 0, 2).reshape(s_, ORDER * pitch)
    top = table.astype(jnp.bfloat16)
    rest = (table - top.astype(np.float32)).astype(jnp.bfloat16)
    table = jnp.asarray(np.concatenate([top, rest], 0))
    early = stations <= s_
    groups = stations if early else s_
    chosen = station_of if early else jnp.arange(s_, dtype=jnp.int32)
    modes = jnp.asarray(radial_modes(r_)[:WALL_SPAN].astype(np.float32))
    pick = (wall_index[:, None] == jnp.arange(WALL_SPAN)[None, :]).astype(jnp.float32)
    values = jnp.dot(pick, modes, precision=PRECISE)
    rates = jnp.asarray(radial_rates(r_))[None, :]
    tall_rows = ORDER * groups

    def kernel(s_in, near, far, tab, station, rate, value, base, out, parts, high, low, terms, old, new):
        k = pl.program_id(0)

        @pl.when(k == 0)
        def _():
            pick = (lax.broadcasted_iota(jnp.int32, (groups, s_), 0) == station[...]).astype(jnp.bfloat16)
            whole = jnp.dot(jnp.concatenate([pick, pick], axis=1), tab[...], preferred_element_type=jnp.float32)
            for j in range(ORDER):
                top, rest = split(whole[:, j * pitch : j * pitch + rows])
                parts[j * groups : (j + 1) * groups] = top
                parts[tall_rows + j * groups : tall_rows + (j + 1) * groups] = rest

        for i in range(TILE):
            own = s_in[i]
            before, at_low, at_high, after = slab_parts(own, near[i], far[i], s_)
            slab = jnp.concatenate(
                [before, own[:TILE] + at_low]
                + ([own[TILE : s_ - TILE]] if s_ > 2 * TILE else [])
                + [own[s_ - TILE : s_] + at_high, after],
                0,
            )
            top, rest = split(slab)
            high[:, i * r_ : (i + 1) * r_] = top
            low[:, i * r_ : (i + 1) * r_] = rest
        one = jnp.dot(parts[...], high[...], preferred_element_type=jnp.float32)
        two = jnp.dot(parts[:tall_rows], low[...], preferred_element_type=jnp.float32)
        terms[k] = one[:tall_rows] + one[tall_rows:] + two

        @pl.when(k == steps - 1)
        def _():
            zero = jnp.zeros((groups, r_), jnp.float32)
            for ref in (old, new):
                ref[0] = zero
                ref[wide + 1] = zero
            first = (ORDER - 1) * groups

            def start(c, _):
                for i in range(TILE):
                    old[c * TILE + i + 1] = terms[c, first : first + groups, i * r_ : (i + 1) * r_]
                return 0

            lax.fori_loop(0, steps, start, 0)
            source, target = old, new
            for j in range(ORDER - 2, -1, -1):

                def level(c, _, j=j, source=source, target=target):
                    for i in range(TILE):
                        t = c * TILE + i + 1
                        target[t] = (
                            source[t - 1]
                            + source[t + 1]
                            + rate[...] * source[t]
                            + terms[c, j * groups : (j + 1) * groups, i * r_ : (i + 1) * r_]
                        )
                    return 0

                lax.fori_loop(0, steps, level, 0)
                source, target = target, source
            ones = jnp.ones((2 * r_, NA), jnp.bfloat16)

            def gather(c, total):
                for i in range(TILE):
                    t = c * TILE + i
                    product = source[t + LEAD + 1] * value[pl.ds(t, 1), :]
                    top, rest = split(product)
                    sums = jnp.dot(
                        jnp.concatenate([top, rest], axis=1), ones, preferred_element_type=jnp.float32
                    )
                    total = total + sums * base[pl.ds(t, 1), :]
                return total

            out[...] = lax.fori_loop(0, t_ // TILE, gather, jnp.zeros((groups, NA), jnp.float32))

    tile = pl.pallas_call(
        kernel,
        grid=(steps,),
        in_specs=[
            pl.BlockSpec((TILE, tall, r_), lambda k: (k, 0, 0)),
            pl.BlockSpec((TILE, TILE, r_), lambda k: (k, 0, 0)),
            pl.BlockSpec((TILE, TILE, r_), lambda k: (k, 0, 0)),
            pl.BlockSpec((2 * s_, ORDER * pitch), lambda k: (0, 0)),
            pl.BlockSpec((1, s_), lambda k: (0, 0)),
            pl.BlockSpec((1, r_), lambda k: (0, 0)),
            pl.BlockSpec((t_, r_), lambda k: (0, 0)),
            pl.BlockSpec((t_, NA), lambda k: (0, 0)),
        ],
        out_specs=pl.BlockSpec((groups, NA), lambda k: (0, 0)),
        out_shape=jax.ShapeDtypeStruct((groups, NA), jnp.float32),
        scratch_shapes=[
            pltpu.VMEM((2 * tall_rows, rows), jnp.bfloat16),
            pltpu.VMEM((rows, TILE * r_), jnp.bfloat16),
            pltpu.VMEM((rows, TILE * r_), jnp.bfloat16),
            pltpu.VMEM((steps, tall_rows, TILE * r_), jnp.float32),
            pltpu.VMEM((wide + 2, groups, r_), jnp.float32),
            pltpu.VMEM((wide + 2, groups, r_), jnp.float32),
        ],
        compiler_params=pltpu.CompilerParams(vmem_limit_bytes=56 << 20),
        name="wall",
    )(s_ext, pack_l, pack_r, table, chosen[None, :], rates, values, basis)
    if not early:
        select = (station_of[:, None] == jnp.arange(stations)[None, :]).astype(jnp.float32)
        tile = jnp.dot(select.T, tile, precision=PRECISE)
    return tile


def azimuth_basis(first_cell, cells, total):
    column = jnp.arange(NA)
    upper = column >= NA // 2
    harmonic = jnp.where(upper, column - NA // 2 + 1, column)
    index = first_cell + jnp.arange(cells)
    phase = index[:, None] * harmonic[None, :] % total
    angle = 2.0 * math.pi / total * phase.astype(jnp.float32)
    return jnp.where(upper[None, :], jnp.sin(angle), jnp.cos(angle))


def bin_weights(scale):
    column = jnp.arange(NF)
    upper = column >= NF // 2
    harmonic = jnp.where(upper, column - NF // 2 + 1, column)
    phase = jnp.arange(NBIN)[:, None] * harmonic[None, :] % NBIN
    angle = 2.0 * math.pi / NBIN * phase.astype(jnp.float32)
    return jnp.where(upper[None, :], jnp.sin(angle), jnp.cos(angle)) * scale


def send(x, spans, planes, by_span, by_plane):
    pairs = []
    for i in range(spans):
        for j in range(planes):
            to = ((i + by_span) % spans) * planes + (j + by_plane) % planes
            pairs.append((i * planes + j, to))
    return lax.ppermute(x, ("span", "plane"), pairs)


def exchange(s_ext, zr, zl, spans, planes, span_cells, theta_cells):
    edge = ORDER + 1
    first = LEAD - 1
    last = LEAD + theta_cells - ORDER
    after = LEAD - ORDER
    before = LEAD + theta_cells - 1

    def planes_of(z, step):
        mid = send(z, spans, planes, step, 0)
        low = send(z[last : last + edge], spans, planes, step, 1)
        high = send(z[first : first + edge], spans, planes, step, -1)
        total = mid.shape[0]
        low = jnp.pad(low, ((after, total - after - edge), (0, 0), (0, 0)))
        high = jnp.pad(high, ((before, total - before - edge), (0, 0), (0, 0)))
        return mid + low + high

    low = send(s_ext[last : last + edge], spans, planes, 0, 1)
    high = send(s_ext[first : first + edge], spans, planes, 0, -1)
    from_left = planes_of(zr, 1)
    from_right = planes_of(zl, -1)
    hop = 1
    while hop < spans and np.any(hop_table(hop * span_cells)):
        table = hop_table(hop * span_cells)
        left_table = np.zeros((TILE, TILE), np.float32)
        left_table[: TILE - ORDER - 1 : -1, [0, 7, 6, 5, 4, 3]] = table
        right_table = np.zeros((TILE, TILE), np.float32)
        right_table[:ORDER, [7, 0, 1, 2, 3, 4]] = table
        far_left = planes_of(zr, hop + 1)
        far_right = planes_of(zl, -hop - 1)
        from_left = from_left + jnp.einsum("bd,adr->abr", left_table, far_left, precision=PRECISE)
        from_right = from_right + jnp.einsum("bd,adr->abr", right_table, far_right, precision=PRECISE)
        hop += 1
    s_ext = s_ext.at[after : after + edge].add(low).at[before : before + edge].add(high)
    return s_ext, from_left, from_right


def share(rows, spans, planes):
    each = rows.shape[0]
    here = lax.axis_index("plane")
    whole = jnp.zeros((planes,) + rows.shape, rows.dtype)
    order = jnp.arange(planes)[:, None, None]
    for step in range(planes):
        piece = rows if step == 0 else send(rows, spans, planes, 0, step)
        whole = jnp.where(order == (here - step) % planes, piece[None], whole)
    return whole.reshape(planes * each, rows.shape[1])


def local(velocity, wall_history, phase_bin, station_of, wall_index, spans, planes):
    _, span_cells, theta_cells, _ = velocity.shape
    total_theta = theta_cells * planes
    stations = ST_DEV * spans
    basis = azimuth_basis(lax.axis_index("plane") * theta_cells, theta_cells, total_theta)
    s_ext, zr, zl = source_call(velocity)
    tiles = bins_call(wall_history, phase_bin, station_of, basis, stations)
    s_ext, pack_l, pack_r = exchange(s_ext, zr, zl, spans, planes, span_cells, theta_cells)
    wall = wall_call(s_ext, pack_l, pack_r, station_of, wall_index, basis, stations)
    newest = (jnp.arange(NBIN) == phase_bin[-1]).astype(jnp.float32)
    tiles = tiles + newest[None, :, None] * wall[:, None, :]
    each = stations // (spans * planes)
    parts = lax.all_to_all(tiles, ("span", "plane"), split_axis=0, concat_axis=0, tiled=True)
    corrected, pressure = project_call(s_ext, pack_l, pack_r, velocity)
    parts, pressure = lax.optimization_barrier((parts, pressure))
    held = jnp.sum(parts.reshape(spans * planes, each, NBIN, NA), axis=0)
    weights = bin_weights(1.0 / math.sqrt(total_theta * (wall_history.shape[0] + 1)))
    mine = jnp.einsum("sba,bf->saf", held, weights, precision=PRECISE).reshape(each, NA * NF)
    coefficients = share(mine, spans, planes)
    return corrected, pressure, coefficients


def solution(mesh):
    spans = mesh.shape["span"]
    planes = mesh.shape["plane"]
    in_specs = (
        P(None, "span", "plane", None),
        P(None, "span", "plane"),
        P(),
        P("span"),
        P("plane"),
    )
    out_specs = (P(None, "span", "plane", None), P("span", "plane", None), P("span", None))

    def body(*args):
        return local(*args, spans, planes)

    return jax.shard_map(body, mesh=mesh, in_specs=in_specs, out_specs=out_specs, check_vma=False)
```

```python
import math

import jax
import jax.numpy as jnp
import numpy as np
from jax import lax
from jax.experimental import pallas as pl
from jax.experimental.pallas import tpu as pltpu
from jax.sharding import PartitionSpec as P

NZ = 1024
NA = 128
NF = 64
NBIN = 64
ITERS = 4
WALL_SPAN = 8
ST_DEV = 4
ORDER = ITERS + 1
TILE = 8
LEAD = 9
RHO = 3.0 - 2.0 * math.sqrt(2.0)
PRECISE = lax.Precision.HIGHEST


def representable(table):
    table = np.asarray(table, np.float64)
    return np.where(np.abs(table) < np.finfo(np.float32).tiny, 0.0, table).astype(np.float32)


def inverse_entry(distance, order=ORDER):
    j = order - 1
    return RHO ** (order + distance) * sum(
        math.comb(j + i, j) * math.comb(j + distance + i, j) * RHO ** (2 * i) for i in range(40)
    )


def carry_weight(node, distance):
    basis = 1.0
    for other in range(ORDER):
        if other != node:
            basis *= (distance - other) / (node - other)
    return RHO ** (distance - node) * basis


def carry_table(cells):
    return representable([[carry_weight(b, d) for d in range(cells)] for b in range(ORDER)])


def hop_table(offset):
    return representable([[carry_weight(b, offset + d) for d in range(-1, ORDER)] for b in range(ORDER)])


def radial_modes(cells):
    index = np.arange(1, cells + 1)
    return math.sqrt(2.0 / (cells + 1)) * np.sin(np.pi * np.outer(index, index) / (cells + 1))


def radial_rates(cells):
    return (2.0 * np.cos(np.pi * np.arange(1, cells + 1) / (cells + 1))).astype(np.float32)


def radial_step(cells):
    return 0.5 * (np.eye(cells, k=-1) - np.eye(cells, k=1))


def stacked(table):
    table = np.asarray(table, np.float32)
    top = table.astype(jnp.bfloat16)
    rest = (table - top.astype(np.float32)).astype(jnp.bfloat16)
    return np.concatenate([top, top, rest], 0)


def span_rows(cells):
    return cells + 3 * TILE


def solve_table(cells):
    rows = span_rows(cells)
    table = np.zeros((cells + TILE, rows))
    entries = [inverse_entry(d) for d in range(cells + 2 * TILE)]
    for i in range(cells + 2):
        for z in range(-ORDER - ITERS, cells + ORDER + ITERS):
            table[(i - 1) % (cells + TILE), (z + TILE) % rows] = entries[abs(i - 1 - z)]
    return representable(table)


def wall_hops(cells):
    hops = 1
    while representable([inverse_entry(hops * cells, j + 1) for j in range(ORDER)]).any():
        hops += 1
    return hops


def wall_table(cells, hops):
    table = np.zeros(((2 * hops + 1) * cells, ORDER, cells + TILE))
    for j in range(ORDER):
        entries = np.array([inverse_entry(d, j + 1) for d in range((hops + 1) * cells + 2)])
        targets = np.arange((2 * hops + 1) * cells) - hops * cells
        for z in range(-1, cells + 1):
            table[:, j, z % (cells + TILE)] = entries[np.abs(targets - z)]
    return representable(table)


def split(x):
    high = x.astype(jnp.bfloat16)
    low = (x - high.astype(jnp.float32)).astype(jnp.bfloat16)
    return high, low


def triple(x):
    high, low = split(x)
    return jnp.concatenate([high, low, high], axis=1)


def source_call(velocity):
    _, s_, t_, r_ = velocity.shape
    wide = t_ + 2 * TILE
    blocks = t_ // TILE
    tall = s_ + TILE
    modes = radial_modes(r_)
    both = jnp.asarray(np.concatenate([stacked(-radial_step(r_) @ modes), stacked(modes)], 0))
    carry = carry_table(s_)
    table = np.zeros((2 * TILE, s_), np.float32)
    for b in range(ORDER):
        table[TILE - 1 - b] = carry[b, ::-1]
        table[TILE + b] = carry[b]
    top = table.astype(jnp.bfloat16)
    rest = (table - top.astype(np.float32)).astype(jnp.bfloat16)
    table = jnp.asarray(np.concatenate([top, rest], 0))

    def kernel(radial, turn, along, tab, both_ref, s_out, zr, zl, keep, hold, lhs, high, low):
        k = pl.program_id(0)

        @pl.when(k == 0)
        def _():
            keep[...] = jnp.zeros_like(keep)
            hold[...] = jnp.zeros_like(hold)
            s_out[...] = jnp.zeros_like(s_out)
            zr[...] = jnp.zeros_like(zr)
            zl[...] = jnp.zeros_like(zl)

        @pl.when(k > 0)
        def _():
            inside = k <= blocks
            pad = jnp.zeros((TILE, r_), jnp.float32)
            for i in range(TILE):
                at = pl.ds(i, s_, stride=TILE)
                x0, x1, x2 = radial[at, :], turn[at, :], along[at, :]
                x0 = jnp.where(inside, x0, 0.0)
                x1 = jnp.where(inside, x1, 0.0)
                x2 = jnp.concatenate([jnp.where(inside, x2, 0.0), pad], 0)
                across = jnp.concatenate([0.5 * (keep[0] - x1), pad], 0)
                lhs[i * tall : (i + 1) * tall, 3 * r_ :] = triple(hold[...] + across)
                hold[...] = 0.5 * (pltpu.roll(x2, 1, 0) - pltpu.roll(x2, tall - 1, 0))
                keep[0] = keep[1]
                keep[1] = x1
                lhs[i * tall : (i + 1) * tall, : 3 * r_] = triple(jnp.concatenate([keep[2], pad], 0))
                keep[2] = x0
            value = jnp.dot(lhs[...], both_ref[...], preferred_element_type=jnp.float32)
            for i in range(TILE):
                own = value[i * tall : (i + 1) * tall]
                s_out[i] = own
                top, rest = split(own[:s_])
                high[:, i * r_ : (i + 1) * r_] = top
                low[:, i * r_ : (i + 1) * r_] = rest
            one = jnp.dot(tab[...], high[...], preferred_element_type=jnp.float32)
            two = jnp.dot(tab[: 2 * TILE], low[...], preferred_element_type=jnp.float32)
            planes = one[: 2 * TILE] + one[2 * TILE :] + two
            row = lax.broadcasted_iota(jnp.int32, (TILE, r_), 0)
            for i in range(TILE):
                edge = s_out[i, s_:]
                here = planes[:, i * r_ : (i + 1) * r_]
                zr[i] = here[:TILE] + jnp.where(row == 0, edge, 0.0)
                zl[i] = here[TILE:] + jnp.where(row == TILE - 1, edge, 0.0)

    def part(axis):
        return pl.BlockSpec((1, s_, TILE, r_), lambda k: (axis, 0, jnp.clip(k - 1, 0, blocks - 1), 0))

    def flat(ref):
        return ref.reshape(s_ * TILE, r_)

    def body(x0, x1, x2, *refs):
        kernel(flat(x0.at[0]), flat(x1.at[0]), flat(x2.at[0]), *refs)

    return pl.pallas_call(
        body,
        grid=(wide // TILE,),
        in_specs=[
            part(0),
            part(1),
            part(2),
            pl.BlockSpec((4 * TILE, s_), lambda k: (0, 0)),
            pl.BlockSpec((6 * r_, r_), lambda k: (0, 0)),
        ],
        out_specs=[
            pl.BlockSpec((TILE, tall, r_), lambda k: (k, 0, 0)),
            pl.BlockSpec((TILE, TILE, r_), lambda k: (k, 0, 0)),
            pl.BlockSpec((TILE, TILE, r_), lambda k: (k, 0, 0)),
        ],
        out_shape=[
            jax.ShapeDtypeStruct((wide, tall, r_), jnp.float32),
            jax.ShapeDtypeStruct((wide, TILE, r_), jnp.float32),
            jax.ShapeDtypeStruct((wide, TILE, r_), jnp.float32),
        ],
        scratch_shapes=[
            pltpu.VMEM((3, s_, r_), jnp.float32),
            pltpu.VMEM((tall, r_), jnp.float32),
            pltpu.VMEM((TILE * tall, 6 * r_), jnp.bfloat16),
            pltpu.VMEM((s_, TILE * r_), jnp.bfloat16),
            pltpu.VMEM((s_, TILE * r_), jnp.bfloat16),
        ],
        compiler_params=pltpu.CompilerParams(vmem_limit_bytes=40 << 20),
        name="source",
    )(velocity, velocity, velocity, table, both)


def bins_call(wall_history, phase_bin, station_of, basis, stations):
    h, s_, t_ = wall_history.shape
    step = max(d for d in range(1, 52) if h % d == 0)
    pair = 2
    def kernel(bins, x, station, base, out, acc):
        c = pl.program_id(0)

        @pl.when(c == 0)
        def _():
            acc[...] = jnp.zeros_like(acc)

        for i in range(step):
            b = bins[c * step + i]
            acc[b] += x[i]

        @pl.when(c == h // step - 1)
        def _():
            high, low = split(base[...])
            stack = jnp.concatenate([high, high, low], 0)
            pick = (lax.broadcasted_iota(jnp.int32, (stations, s_), 0) == station[...]).astype(jnp.bfloat16)

            def body(j, _):
                held = jnp.concatenate([acc[j * pair + q] for q in range(pair)], axis=1)
                top, rest = split(held)
                rows = jnp.dot(pick, top, preferred_element_type=jnp.float32) + jnp.dot(
                    pick, rest, preferred_element_type=jnp.float32
                )
                both = jnp.concatenate([rows[:, q * t_ : (q + 1) * t_] for q in range(pair)], axis=0)
                top, rest = split(both)
                tile = jnp.dot(
                    jnp.concatenate([top, rest, top], axis=1), stack, preferred_element_type=jnp.float32
                )
                for q in range(pair):
                    out[pl.ds(j * pair + q, stations, stride=NBIN), :] = tile[q * stations : (q + 1) * stations]
                return 0

            lax.fori_loop(0, NBIN // pair, body, 0, unroll=4)

    tiles = pl.pallas_call(
        kernel,
        grid_spec=pltpu.PrefetchScalarGridSpec(
            num_scalar_prefetch=1,
            grid=(h // step,),
            in_specs=[
                pl.BlockSpec((step, s_, t_), lambda c, bins: (c, 0, 0)),
                pl.BlockSpec((1, s_), lambda c, bins: (0, 0)),
                pl.BlockSpec((t_, NA), lambda c, bins: (0, 0)),
            ],
            out_specs=pl.BlockSpec((stations * NBIN, NA), lambda c, bins: (0, 0)),
            scratch_shapes=[pltpu.VMEM((NBIN, s_, t_), jnp.float32)],
        ),
        out_shape=jax.ShapeDtypeStruct((stations * NBIN, NA), jnp.float32),
        compiler_params=pltpu.CompilerParams(vmem_limit_bytes=40 << 20),
        name="bins",
    )(phase_bin, wall_history, station_of[None, :], basis)
    return tiles.reshape(stations, NBIN, NA)


def slab_parts(own, low, high, cells):
    row = lax.broadcasted_iota(jnp.int32, (TILE, own.shape[-1]), 0)
    edge = own[cells:]
    before = jnp.where(row >= TILE - ORDER, low, 0.0) + jnp.where(row == TILE - 1, edge, 0.0)
    after = jnp.where(row < ORDER, high, 0.0) + jnp.where(row == 0, edge, 0.0)
    return before, jnp.where(row == 0, low, 0.0), jnp.where(row == TILE - 1, high, 0.0), after


def project_call(s_ext, pack_l, pack_r, velocity):
    _, s_, t_, r_ = velocity.shape
    wide = t_ + 2 * TILE
    rows = span_rows(s_)
    held = rows + (-rows) % (2 * TILE)
    out_rows = s_ + TILE
    steps = wide // TILE
    table = np.pad(solve_table(s_), ((0, 0), (0, held - rows)))
    top = table.astype(jnp.bfloat16)
    rest = (table - top.astype(np.float32)).astype(jnp.bfloat16)
    table = jnp.asarray(np.concatenate([top, rest], 0))
    modes = radial_modes(r_)
    back = jnp.asarray(np.concatenate([stacked(modes), stacked(modes @ radial_step(r_))], 1))
    rates = jnp.asarray(radial_rates(r_))[None, :]
    slots = TILE + 2

    share_ = TILE // ITERS

    def kernel(s_in, near, far, v0, v1, v2, tab, turn, rate, c0, c1, c2, pressure, *scratch):
        a0, a1, a2, a3, w1, w2, w3, high, low, ready_high, ready_low, pot, rad = scratch
        k = pl.program_id(0)
        levels_a = [a0, a1, a2, a3]
        levels_w = [a0, w1, w2, w3]

        @pl.when(k == 0)
        def _():
            for ref in (a0, a1, a2, a3, w1, w2, w3):
                ref[TILE:slots] = jnp.zeros((2, rows, r_), jnp.float32)
            a0[:, rows - TILE :] = jnp.zeros((slots, TILE, r_), jnp.float32)
            high[...] = jnp.zeros_like(high)
            low[...] = jnp.zeros_like(low)
            pot[...] = jnp.zeros_like(pot)
            rad[...] = jnp.zeros_like(rad)

        for ref in (a0, a1, a2, a3, w1, w2, w3):
            ref[0:2] = ref[TILE:slots]
        pot[:TILE] = pot[TILE:]
        rad[:TILE] = rad[TILE:]
        ready_high[...] = high[...]
        ready_low[...] = low[...]

        for i in range(TILE):
            own = s_in[i]
            before, at_low, at_high, after = slab_parts(own, near[i], far[i], s_)
            a0[i + 2, 0:TILE] = before
            a0[i + 2, TILE : 2 * TILE] = own[:TILE] + at_low
            if s_ > 2 * TILE:
                a0[i + 2, 2 * TILE : s_] = own[TILE : s_ - TILE]
            a0[i + 2, s_ : s_ + TILE] = own[s_ - TILE : s_] + at_high
            a0[i + 2, s_ + TILE : s_ + 2 * TILE] = after

        for n in range(1, ITERS + 1):
            past, weighted = levels_a[n - 1], levels_w[n - 1]
            columns = slice((n - 1) * share_ * r_, n * share_ * r_)
            one = jnp.dot(tab[...], ready_high[:, columns], preferred_element_type=jnp.float32)
            two = jnp.dot(tab[:out_rows], ready_low[:, columns], preferred_element_type=jnp.float32)
            solved = one[:out_rows] + one[out_rows:] + two
            for i in range(TILE):
                total = past[i] + past[i + 2] + rate[...] * past[i + 1]
                mid = weighted[i + 1]
                value = 6.0 * mid - (pltpu.roll(mid, 1, 0) + pltpu.roll(mid, rows - 1, 0)) + total
                if n < ITERS:
                    levels_a[n][i + 2] = total
                    levels_w[n][i + 2] = value
                else:
                    value = jnp.concatenate([value, jnp.zeros((held - rows, r_), jnp.float32)], 0)
                    top_part, rest_part = split(value)
                    high[:, i * r_ : (i + 1) * r_] = top_part
                    low[:, i * r_ : (i + 1) * r_] = rest_part
            solved = jnp.concatenate([solved[:, i * r_ : (i + 1) * r_] for i in range(share_)], 0)
            solved = jnp.dot(triple(solved), turn[...], preferred_element_type=jnp.float32)
            for i in range(share_):
                pot[TILE + (n - 1) * share_ + i] = solved[i * out_rows : (i + 1) * out_rows, :r_]
                rad[TILE + (n - 1) * share_ + i] = solved[i * out_rows : i * out_rows + s_, r_:]
            for i in range((n - 1) * share_, n * share_):
                at = LEAD - ORDER + 1 + i
                out = pl.ds(i, s_, stride=TILE)
                mid = pot[at]
                along = pltpu.roll(mid, out_rows - 1, 0) - pltpu.roll(mid, 1, 0)
                pressure[out, :] = mid[:s_]
                c0[out, :] = v0[out, :] - rad[at]
                c1[out, :] = v1[out, :] - 0.5 * (pot[at + 1, :s_] - pot[at - 1, :s_])
                c2[out, :] = v2[out, :] - 0.5 * along[:s_]

    def flat(ref):
        return ref.reshape(s_ * TILE, r_)

    def body(s_in, near, far, v, tab, turn, rate, corrected, pressure, *scratch):
        parts = [flat(v.at[i]) for i in range(3)]
        outs = [flat(corrected.at[i]) for i in range(3)]
        kernel(s_in, near, far, *parts, tab, turn, rate, *outs, flat(pressure), *scratch)

    at = lambda k: jnp.maximum(k - 3, 0)
    of = lambda k: jnp.minimum(k, steps - 1)
    slab = pltpu.VMEM((slots, rows, r_), jnp.float32)
    return pl.pallas_call(
        body,
        grid=(steps + 1,),
        in_specs=[
            pl.BlockSpec((TILE, s_ + TILE, r_), lambda k: (of(k), 0, 0)),
            pl.BlockSpec((TILE, TILE, r_), lambda k: (of(k), 0, 0)),
            pl.BlockSpec((TILE, TILE, r_), lambda k: (of(k), 0, 0)),
            pl.BlockSpec((3, s_, TILE, r_), lambda k: (0, 0, at(k), 0)),
            pl.BlockSpec((2 * out_rows, held), lambda k: (0, 0)),
            pl.BlockSpec((3 * r_, 2 * r_), lambda k: (0, 0)),
            pl.BlockSpec((1, r_), lambda k: (0, 0)),
        ],
        out_specs=[
            pl.BlockSpec((3, s_, TILE, r_), lambda k: (0, 0, at(k), 0)),
            pl.BlockSpec((s_, TILE, r_), lambda k: (0, at(k), 0)),
        ],
        out_shape=[
            jax.ShapeDtypeStruct(velocity.shape, jnp.float32),
            jax.ShapeDtypeStruct(velocity.shape[1:], jnp.float32),
        ],
        scratch_shapes=[slab] * 7
        + [pltpu.VMEM((held, TILE * r_), jnp.bfloat16)] * 4
        + [pltpu.VMEM((2 * TILE, out_rows, r_), jnp.float32), pltpu.VMEM((2 * TILE, s_, r_), jnp.float32)],
        compiler_params=pltpu.CompilerParams(vmem_limit_bytes=56 << 20),
        name="project",
    )(s_ext, pack_l, pack_r, velocity, table, back, rates)


def wall_call(s_ext, near_stations, near_walls, near_basis, stations):
    cells = s_ext.shape[1] - TILE
    table = wall_table(cells, wall_hops(cells))
    targets = near_stations.shape[0]
    if stations <= targets:
        return wall_part(s_ext, table, near_stations, near_walls, near_basis, stations)
    batch = max(d for d in range(TILE, 6 * TILE + 1, TILE) if targets % d == 0)
    index = jnp.arange(batch, dtype=jnp.int32)
    planes = [
        wall_part(s_ext, table[i : i + batch], index, near_walls, near_basis, batch) for i in range(0, targets, batch)
    ]
    select = (near_stations[:, None] == jnp.arange(stations)[None, :]).astype(jnp.float32)
    return jnp.dot(select.T, jnp.concatenate(planes, 0), precision=PRECISE)


def wall_part(s_ext, table, chosen, near_walls, near_basis, groups):
    wide, tall, r_ = s_ext.shape
    s_ = tall - TILE
    rows = tall + (-tall) % (2 * TILE)
    chunks = wide // TILE
    group = max(d for d in range(1, 4) if chunks % d == 0)
    steps = chunks // group
    targets = chosen.shape[0]
    pitch = rows + (-rows) % r_
    table = np.pad(table, ((0, 0), (0, 0), (0, pitch - tall))).reshape(targets, ORDER * pitch)
    top = table.astype(jnp.bfloat16)
    rest = (table - top.astype(np.float32)).astype(jnp.bfloat16)
    table = jnp.asarray(np.concatenate([top, rest], 0))
    modes = jnp.asarray(radial_modes(r_)[:WALL_SPAN].astype(np.float32))
    pick = (near_walls[:, None] == jnp.arange(WALL_SPAN)[None, :]).astype(jnp.float32)
    values = jnp.dot(pick, modes, precision=PRECISE)
    rates = jnp.asarray(radial_rates(r_))[None, :]
    tall_rows = ORDER * groups

    def kernel(s_in, tab, station, rate, value, base, out, parts, high, low, terms, old, new):
        k = pl.program_id(0)

        @pl.when(k == 0)
        def _():
            pick = (lax.broadcasted_iota(jnp.int32, (groups, targets), 0) == station[...]).astype(jnp.bfloat16)
            whole = jnp.dot(jnp.concatenate([pick, pick], axis=1), tab[...], preferred_element_type=jnp.float32)
            for j in range(ORDER):
                top, rest = split(whole[:, j * pitch : j * pitch + rows])
                parts[j * groups : (j + 1) * groups] = top
                parts[tall_rows + j * groups : tall_rows + (j + 1) * groups] = rest

        for c in range(group):
            for i in range(TILE):
                slab = s_in[c * TILE + i]
                if rows > tall:
                    slab = jnp.concatenate([slab, jnp.zeros((rows - tall, r_), jnp.float32)], 0)
                top, rest = split(slab)
                high[c, :, i * r_ : (i + 1) * r_] = top
                low[c, :, i * r_ : (i + 1) * r_] = rest
            one = jnp.dot(parts[...], high[c], preferred_element_type=jnp.float32)
            two = jnp.dot(parts[:tall_rows], low[c], preferred_element_type=jnp.float32)
            terms[k * group + c] = one[:tall_rows] + one[tall_rows:] + two

        @pl.when(k == steps - 1)
        def _():
            zero = jnp.zeros((groups, r_), jnp.float32)
            for ref in (old, new):
                ref[0] = zero
                ref[wide + 1] = zero
            first = (ORDER - 1) * groups

            def start(c, _):
                for i in range(TILE):
                    old[c * TILE + i + 1] = terms[c, first : first + groups, i * r_ : (i + 1) * r_]
                return 0

            lax.fori_loop(0, chunks, start, 0)
            source, target = old, new
            for j in range(ORDER - 2, -1, -1):

                def level(c, _, j=j, source=source, target=target):
                    for i in range(TILE):
                        t = c * TILE + i + 1
                        target[t] = (
                            source[t - 1]
                            + source[t + 1]
                            + rate[...] * source[t]
                            + terms[c, j * groups : (j + 1) * groups, i * r_ : (i + 1) * r_]
                        )
                    return 0

                lax.fori_loop(0, chunks, level, 0)
                source, target = target, source
            ones = jnp.ones((2 * r_, NA), jnp.bfloat16)

            def gather(c, total):
                for i in range(TILE):
                    t = c * TILE + i
                    product = source[t + 1] * value[pl.ds(t, 1), :]
                    top, rest = split(product)
                    sums = jnp.dot(
                        jnp.concatenate([top, rest], axis=1), ones, preferred_element_type=jnp.float32
                    )
                    total = total + sums * base[pl.ds(t, 1), :]
                return total

            out[...] = lax.fori_loop(0, chunks, gather, jnp.zeros((groups, NA), jnp.float32))

    tile = pl.pallas_call(
        kernel,
        grid=(steps,),
        in_specs=[
            pl.BlockSpec((group * TILE, tall, r_), lambda k: (k, 0, 0)),
            pl.BlockSpec((2 * targets, ORDER * pitch), lambda k: (0, 0)),
            pl.BlockSpec((1, targets), lambda k: (0, 0)),
            pl.BlockSpec((1, r_), lambda k: (0, 0)),
            pl.BlockSpec((wide, r_), lambda k: (0, 0)),
            pl.BlockSpec((wide, NA), lambda k: (0, 0)),
        ],
        out_specs=pl.BlockSpec((groups, NA), lambda k: (0, 0)),
        out_shape=jax.ShapeDtypeStruct((groups, NA), jnp.float32),
        scratch_shapes=[
            pltpu.VMEM((2 * tall_rows, rows), jnp.bfloat16),
            pltpu.VMEM((group, rows, TILE * r_), jnp.bfloat16),
            pltpu.VMEM((group, rows, TILE * r_), jnp.bfloat16),
            pltpu.VMEM((chunks, tall_rows, TILE * r_), jnp.float32),
            pltpu.VMEM((wide + 2, groups, r_), jnp.float32),
            pltpu.VMEM((wide + 2, groups, r_), jnp.float32),
        ],
        compiler_params=pltpu.CompilerParams(vmem_limit_bytes=56 << 20),
        name="wall",
    )(s_ext, table, chosen[None, :], rates, values, near_basis)
    return tile


def azimuth_basis(first_cell, cells, total):
    column = jnp.arange(NA)
    upper = column >= NA // 2
    harmonic = jnp.where(upper, column - NA // 2 + 1, column)
    index = first_cell + jnp.arange(cells)
    phase = index[:, None] * harmonic[None, :] % total
    angle = 2.0 * math.pi / total * phase.astype(jnp.float32)
    return jnp.where(upper[None, :], jnp.sin(angle), jnp.cos(angle))


def bin_weights(scale):
    column = jnp.arange(NF)
    upper = column >= NF // 2
    harmonic = jnp.where(upper, column - NF // 2 + 1, column)
    phase = jnp.arange(NBIN)[:, None] * harmonic[None, :] % NBIN
    angle = 2.0 * math.pi / NBIN * phase.astype(jnp.float32)
    return jnp.where(upper[None, :], jnp.sin(angle), jnp.cos(angle)) * scale


def send(x, spans, planes, by_span, by_plane):
    pairs = []
    for i in range(spans):
        for j in range(planes):
            to = ((i + by_span) % spans) * planes + (j + by_plane) % planes
            pairs.append((i * planes + j, to))
    return lax.ppermute(x, ("span", "plane"), pairs)


def turn_exchange(s_ext, zr, zl, wall_index, spans, planes):
    theta_cells = wall_index.shape[0]
    tall = s_ext.shape[1]
    edge = ORDER + 1
    wide = s_ext.shape[0]
    first = LEAD - 1
    last = LEAD + theta_cells - ORDER
    after = LEAD - ORDER
    before = LEAD + theta_cells - 1

    def packed(at, walls):
        free = jnp.pad(walls.astype(jnp.float32), (0, zr.shape[2] - ORDER))
        own = zr[at : at + edge]
        own = jnp.where(jnp.arange(TILE)[None, :, None] == 1, free[None, None, :], own)
        return jnp.concatenate([s_ext[at : at + edge], own, zl[at : at + edge]], axis=1)

    low = send(packed(last, wall_index[-ORDER:]), spans, planes, 0, 1)
    high = send(packed(first, wall_index[:ORDER]), spans, planes, 0, -1)

    def unpacked():
        rows = jnp.arange(TILE)[None, :, None] != 1
        whole = []
        for mid, start in ((zr, tall), (zl, tall + TILE)):
            sides = []
            for piece, at in ((low, after), (high, before)):
                piece = piece[:, start : start + TILE]
                if start == tall:
                    piece = jnp.where(rows, piece, 0.0)
                sides.append(jnp.pad(piece, ((at, wide - at - edge), (0, 0), (0, 0))))
            whole.append(mid + sides[0] + sides[1])
        walls = [piece[0, tall + 1, :ORDER].astype(wall_index.dtype) for piece in (low, high)]
        none = jnp.full((wide,), -1, wall_index.dtype)
        walls = jnp.concatenate(
            [none[:after], walls[0], wall_index, walls[1], none[LEAD + theta_cells + ORDER :]], 0
        )
        return whole[0], whole[1], walls

    return low, high, unpacked


def span_exchange(zr, zl, spans, planes, span_cells):
    from_left = [send(zr, spans, planes, 1, 0)]
    from_right = [send(zl, spans, planes, -1, 0)]
    tables = []
    while len(from_left) < spans and np.any(hop_table(len(from_left) * span_cells)):
        table = hop_table(len(from_left) * span_cells)
        left_table = np.zeros((TILE, TILE), np.float32)
        left_table[: TILE - ORDER - 1 : -1, [0, 7, 6, 5, 4, 3]] = table
        right_table = np.zeros((TILE, TILE), np.float32)
        right_table[:ORDER, [7, 0, 1, 2, 3, 4]] = table
        tables.append((left_table, right_table))
        hop = len(from_left) + 1
        from_left.append(send(zr, spans, planes, hop, 0))
        from_right.append(send(zl, spans, planes, -hop, 0))
    return from_left, from_right, tables


def share(rows, spans, planes):
    each = rows.shape[0]
    here = lax.axis_index("plane")
    whole = jnp.zeros((planes,) + rows.shape, rows.dtype)
    order = jnp.arange(planes)[:, None, None]
    for step in range(planes):
        piece = rows if step == 0 else send(rows, spans, planes, 0, step)
        whole = jnp.where(order == (here - step) % planes, piece[None], whole)
    return whole.reshape(planes * each, rows.shape[1])


def local(velocity, wall_history, phase_bin, station_of, wall_index, spans, planes):
    _, span_cells, theta_cells, _ = velocity.shape
    total_theta = theta_cells * planes
    stations = ST_DEV * spans
    wide = theta_cells + 2 * TILE
    hops = wall_hops(span_cells)
    near_basis = azimuth_basis(lax.axis_index("plane") * theta_cells - LEAD, wide, total_theta)
    basis = near_basis[LEAD : LEAD + theta_cells]
    s_own, zr, zl = source_call(velocity)
    station_of, wall_index, s_own = lax.optimization_barrier((station_of, wall_index, s_own))
    low, high, unpacked = turn_exchange(s_own, zr, zl, wall_index, spans, planes)
    sides = [send(station_of, spans, planes, -h, 0) if h else station_of for h in range(-hops, hops + 1)]
    tiles = bins_call(wall_history, phase_bin, station_of, basis, stations)
    zr_wide, zl_wide, near_walls = unpacked()
    zr_wide, zl_wide, near_walls, sides, tiles = lax.optimization_barrier((zr_wide, zl_wide, near_walls, sides, tiles))
    from_left, from_right, tables = span_exchange(zr_wide, zl_wide, spans, planes, span_cells)
    near_stations = jnp.concatenate(sides, 0)
    wall = wall_call(s_own, near_stations, near_walls, near_basis, stations)
    newest = (jnp.arange(NBIN) == phase_bin[-1]).astype(jnp.float32)
    tiles = tiles + newest[None, :, None] * wall[:, None, :]
    from_left, from_right, tiles, s_own = lax.optimization_barrier((from_left, from_right, tiles, s_own))
    tall = span_cells + TILE
    s_ext = s_own.at[LEAD - ORDER : LEAD + 1].add(low[:, :tall])
    s_ext = s_ext.at[LEAD + theta_cells - 1 : LEAD + theta_cells + ORDER].add(high[:, :tall])
    pack_l, pack_r = from_left[0], from_right[0]
    for far_left, far_right, (left_table, right_table) in zip(from_left[1:], from_right[1:], tables):
        pack_l = pack_l + jnp.einsum("bd,adr->abr", left_table, far_left, precision=PRECISE)
        pack_r = pack_r + jnp.einsum("bd,adr->abr", right_table, far_right, precision=PRECISE)
    each = stations // (spans * planes)
    parts = lax.all_to_all(tiles, ("span", "plane"), split_axis=0, concat_axis=0, tiled=True)
    corrected, pressure = project_call(s_ext, pack_l, pack_r, velocity)
    parts, pressure = lax.optimization_barrier((parts, pressure))
    held = jnp.sum(parts.reshape(spans * planes, each, NBIN, NA), axis=0)
    weights = bin_weights(1.0 / math.sqrt(total_theta * (wall_history.shape[0] + 1)))
    mine = jnp.einsum("sba,bf->saf", held, weights, precision=PRECISE).reshape(each, NA * NF)
    coefficients = share(mine, spans, planes)
    return corrected, pressure, coefficients


def solution(mesh):
    spans = mesh.shape["span"]
    planes = mesh.shape["plane"]
    in_specs = (
        P(None, "span", "plane", None),
        P(None, "span", "plane"),
        P(),
        P("span"),
        P("plane"),
    )
    out_specs = (P(None, "span", "plane", None), P("span", "plane", None), P("span", None))

    def body(*args):
        return local(*args, spans, planes)

    return jax.shard_map(body, mesh=mesh, in_specs=in_specs, out_specs=out_specs, check_vma=False)
```

```python
import math

import jax
import jax.numpy as jnp
import numpy as np
from jax import lax
from jax.experimental import pallas as pl
from jax.experimental.pallas import tpu as pltpu
from jax.sharding import PartitionSpec as P

NZ = 1024
NA = 128
NF = 64
NBIN = 64
ITERS = 4
WALL_SPAN = 8
ST_DEV = 4
ORDER = ITERS + 1
TILE = 8
LEAD = 9
RHO = 3.0 - 2.0 * math.sqrt(2.0)
PRECISE = lax.Precision.HIGHEST


def representable(table):
    table = np.asarray(table, np.float64)
    return np.where(np.abs(table) < np.finfo(np.float32).tiny, 0.0, table).astype(np.float32)


def inverse_entry(distance, order=ORDER):
    j = order - 1
    return RHO ** (order + distance) * sum(
        math.comb(j + i, j) * math.comb(j + distance + i, j) * RHO ** (2 * i) for i in range(40)
    )


def carry_weight(node, distance):
    basis = 1.0
    for other in range(ORDER):
        if other != node:
            basis *= (distance - other) / (node - other)
    return RHO ** (distance - node) * basis


def carry_table(cells):
    return representable([[carry_weight(b, d) for d in range(cells)] for b in range(ORDER)])


def hop_table(offset):
    return representable([[carry_weight(b, offset + d) for d in range(-1, ORDER)] for b in range(ORDER)])


def radial_modes(cells):
    index = np.arange(1, cells + 1)
    return math.sqrt(2.0 / (cells + 1)) * np.sin(np.pi * np.outer(index, index) / (cells + 1))


def radial_rates(cells):
    return (2.0 * np.cos(np.pi * np.arange(1, cells + 1) / (cells + 1))).astype(np.float32)


def radial_step(cells):
    return 0.5 * (np.eye(cells, k=-1) - np.eye(cells, k=1))


def stacked(table):
    table = np.asarray(table, np.float32)
    top = table.astype(jnp.bfloat16)
    rest = (table - top.astype(np.float32)).astype(jnp.bfloat16)
    return np.concatenate([top, top, rest], 0)


def span_rows(cells):
    return cells + 3 * TILE


def solve_table(cells):
    rows = span_rows(cells)
    table = np.zeros((cells + TILE, rows))
    entries = [inverse_entry(d) for d in range(cells + 2 * TILE)]
    for i in range(cells + 2):
        for z in range(-ORDER - ITERS, cells + ORDER + ITERS):
            table[(i - 1) % (cells + TILE), (z + TILE) % rows] = entries[abs(i - 1 - z)]
    return representable(table)


def wall_hops(cells):
    hops = 1
    while representable([inverse_entry(hops * cells, j + 1) for j in range(ORDER)]).any():
        hops += 1
    return hops


def wall_table(cells, hops):
    table = np.zeros(((2 * hops + 1) * cells, ORDER, cells + TILE))
    for j in range(ORDER):
        entries = np.array([inverse_entry(d, j + 1) for d in range((hops + 1) * cells + 2)])
        targets = np.arange((2 * hops + 1) * cells) - hops * cells
        for z in range(-1, cells + 1):
            table[:, j, z % (cells + TILE)] = entries[np.abs(targets - z)]
    return representable(table)


def split(x):
    high = x.astype(jnp.bfloat16)
    low = (x - high.astype(jnp.float32)).astype(jnp.bfloat16)
    return high, low


def triple(x):
    high, low = split(x)
    return jnp.concatenate([high, low, high], axis=1)


def source_call(velocity):
    _, s_, t_, r_ = velocity.shape
    wide = t_ + 2 * TILE
    blocks = t_ // TILE
    tall = s_ + TILE
    modes = radial_modes(r_)
    both = jnp.asarray(np.concatenate([stacked(-radial_step(r_) @ modes), stacked(modes)], 0))
    carry = carry_table(s_)
    table = np.zeros((2 * TILE, s_), np.float32)
    for b in range(ORDER):
        table[TILE - 1 - b] = carry[b, ::-1]
        table[TILE + b] = carry[b]
    top = table.astype(jnp.bfloat16)
    rest = (table - top.astype(np.float32)).astype(jnp.bfloat16)
    table = jnp.asarray(np.concatenate([top, rest], 0))

    def kernel(radial, turn, along, tab, both_ref, s_out, zr, zl, keep, hold, lhs, high, low):
        k = pl.program_id(0)

        @pl.when(k == 0)
        def _():
            keep[...] = jnp.zeros_like(keep)
            hold[...] = jnp.zeros_like(hold)
            s_out[...] = jnp.zeros_like(s_out)
            zr[...] = jnp.zeros_like(zr)
            zl[...] = jnp.zeros_like(zl)

        @pl.when(k > 0)
        def _():
            inside = k <= blocks
            pad = jnp.zeros((TILE, r_), jnp.float32)
            for i in range(TILE):
                at = pl.ds(i, s_, stride=TILE)
                x0, x1, x2 = radial[at, :], turn[at, :], along[at, :]
                x0 = jnp.where(inside, x0, 0.0)
                x1 = jnp.where(inside, x1, 0.0)
                x2 = jnp.concatenate([jnp.where(inside, x2, 0.0), pad], 0)
                across = jnp.concatenate([0.5 * (keep[0] - x1), pad], 0)
                lhs[i * tall : (i + 1) * tall, 3 * r_ :] = triple(hold[...] + across)
                hold[...] = 0.5 * (pltpu.roll(x2, 1, 0) - pltpu.roll(x2, tall - 1, 0))
                keep[0] = keep[1]
                keep[1] = x1
                lhs[i * tall : (i + 1) * tall, : 3 * r_] = triple(jnp.concatenate([keep[2], pad], 0))
                keep[2] = x0
            value = jnp.dot(lhs[...], both_ref[...], preferred_element_type=jnp.float32)
            for i in range(TILE):
                own = value[i * tall : (i + 1) * tall]
                s_out[i] = own
                top, rest = split(own[:s_])
                high[:, i * r_ : (i + 1) * r_] = top
                low[:, i * r_ : (i + 1) * r_] = rest
            one = jnp.dot(tab[...], high[...], preferred_element_type=jnp.float32)
            two = jnp.dot(tab[: 2 * TILE], low[...], preferred_element_type=jnp.float32)
            planes = one[: 2 * TILE] + one[2 * TILE :] + two
            row = lax.broadcasted_iota(jnp.int32, (TILE, r_), 0)
            for i in range(TILE):
                edge = s_out[i, s_:]
                here = planes[:, i * r_ : (i + 1) * r_]
                zr[i] = here[:TILE] + jnp.where(row == 0, edge, 0.0)
                zl[i] = here[TILE:] + jnp.where(row == TILE - 1, edge, 0.0)

    def part(axis):
        return pl.BlockSpec((1, s_, TILE, r_), lambda k: (axis, 0, jnp.clip(k - 1, 0, blocks - 1), 0))

    def flat(ref):
        return ref.reshape(s_ * TILE, r_)

    def body(x0, x1, x2, *refs):
        kernel(flat(x0.at[0]), flat(x1.at[0]), flat(x2.at[0]), *refs)

    return pl.pallas_call(
        body,
        grid=(wide // TILE,),
        in_specs=[
            part(0),
            part(1),
            part(2),
            pl.BlockSpec((4 * TILE, s_), lambda k: (0, 0)),
            pl.BlockSpec((6 * r_, r_), lambda k: (0, 0)),
        ],
        out_specs=[
            pl.BlockSpec((TILE, tall, r_), lambda k: (k, 0, 0)),
            pl.BlockSpec((TILE, TILE, r_), lambda k: (k, 0, 0)),
            pl.BlockSpec((TILE, TILE, r_), lambda k: (k, 0, 0)),
        ],
        out_shape=[
            jax.ShapeDtypeStruct((wide, tall, r_), jnp.float32),
            jax.ShapeDtypeStruct((wide, TILE, r_), jnp.float32),
            jax.ShapeDtypeStruct((wide, TILE, r_), jnp.float32),
        ],
        scratch_shapes=[
            pltpu.VMEM((3, s_, r_), jnp.float32),
            pltpu.VMEM((tall, r_), jnp.float32),
            pltpu.VMEM((TILE * tall, 6 * r_), jnp.bfloat16),
            pltpu.VMEM((s_, TILE * r_), jnp.bfloat16),
            pltpu.VMEM((s_, TILE * r_), jnp.bfloat16),
        ],
        compiler_params=pltpu.CompilerParams(vmem_limit_bytes=40 << 20),
        name="source",
    )(velocity, velocity, velocity, table, both)


def bins_call(wall_history, phase_bin, station_of, basis, stations):
    h, s_, t_ = wall_history.shape
    step = max(d for d in range(1, 52) if h % d == 0)
    pair = 4
    def kernel(bins, x, station, base, out, acc):
        c = pl.program_id(0)

        @pl.when(c == 0)
        def _():
            acc[...] = jnp.zeros_like(acc)

        for i in range(step):
            b = bins[c * step + i]
            acc[b] += x[i]

        @pl.when(c == h // step - 1)
        def _():
            high, low = split(base[...])
            stack = jnp.concatenate([high, high, low], 0)
            pick = (lax.broadcasted_iota(jnp.int32, (stations, s_), 0) == station[...]).astype(jnp.bfloat16)

            def body(j, _):
                held = jnp.concatenate([acc[j * pair + q] for q in range(pair)], axis=1)
                top, rest = split(held)
                rows = jnp.dot(pick, top, preferred_element_type=jnp.float32) + jnp.dot(
                    pick, rest, preferred_element_type=jnp.float32
                )
                both = jnp.concatenate([rows[:, q * t_ : (q + 1) * t_] for q in range(pair)], axis=0)
                top, rest = split(both)
                tile = jnp.dot(
                    jnp.concatenate([top, rest, top], axis=1), stack, preferred_element_type=jnp.float32
                )
                for q in range(pair):
                    out[pl.ds(j * pair + q, stations, stride=NBIN), :] = tile[q * stations : (q + 1) * stations]
                return 0

            lax.fori_loop(0, NBIN // pair, body, 0, unroll=4)

    tiles = pl.pallas_call(
        kernel,
        grid_spec=pltpu.PrefetchScalarGridSpec(
            num_scalar_prefetch=1,
            grid=(h // step,),
            in_specs=[
                pl.BlockSpec((step, s_, t_), lambda c, bins: (c, 0, 0)),
                pl.BlockSpec((1, s_), lambda c, bins: (0, 0)),
                pl.BlockSpec((t_, NA), lambda c, bins: (0, 0)),
            ],
            out_specs=pl.BlockSpec((stations * NBIN, NA), lambda c, bins: (0, 0)),
            scratch_shapes=[pltpu.VMEM((NBIN, s_, t_), jnp.float32)],
        ),
        out_shape=jax.ShapeDtypeStruct((stations * NBIN, NA), jnp.float32),
        compiler_params=pltpu.CompilerParams(vmem_limit_bytes=40 << 20),
        name="bins",
    )(phase_bin, wall_history, station_of[None, :], basis)
    return tiles.reshape(stations, NBIN, NA)


def slab_parts(own, low, high, cells):
    row = lax.broadcasted_iota(jnp.int32, (TILE, own.shape[-1]), 0)
    edge = own[cells:]
    before = jnp.where(row >= TILE - ORDER, low, 0.0) + jnp.where(row == TILE - 1, edge, 0.0)
    after = jnp.where(row < ORDER, high, 0.0) + jnp.where(row == 0, edge, 0.0)
    return before, jnp.where(row == 0, low, 0.0), jnp.where(row == TILE - 1, high, 0.0), after


def project_call(s_ext, pack_l, pack_r, velocity):
    _, s_, t_, r_ = velocity.shape
    wide = t_ + 2 * TILE
    rows = span_rows(s_)
    held = rows + (-rows) % (2 * TILE)
    out_rows = s_ + TILE
    steps = wide // TILE
    table = np.pad(solve_table(s_), ((0, 0), (0, held - rows)))
    top = table.astype(jnp.bfloat16)
    rest = (table - top.astype(np.float32)).astype(jnp.bfloat16)
    table = jnp.asarray(np.concatenate([top, rest], 0))
    modes = radial_modes(r_)
    back = jnp.asarray(np.concatenate([stacked(modes), stacked(modes @ radial_step(r_))], 1))
    rates = jnp.asarray(radial_rates(r_))[None, :]
    slots = TILE + 2

    share_ = TILE // ITERS

    def kernel(s_in, near, far, v0, v1, v2, tab, turn, rate, c0, c1, c2, pressure, *scratch):
        a0, a1, a2, a3, w1, w2, w3, high, low, ready_high, ready_low, pot, rad = scratch
        k = pl.program_id(0)
        levels_a = [a0, a1, a2, a3]
        levels_w = [a0, w1, w2, w3]

        @pl.when(k == 0)
        def _():
            for ref in (a0, a1, a2, a3, w1, w2, w3):
                ref[TILE:slots] = jnp.zeros((2, rows, r_), jnp.float32)
            a0[:, rows - TILE :] = jnp.zeros((slots, TILE, r_), jnp.float32)
            high[...] = jnp.zeros_like(high)
            low[...] = jnp.zeros_like(low)
            pot[...] = jnp.zeros_like(pot)
            rad[...] = jnp.zeros_like(rad)

        for ref in (a0, a1, a2, a3, w1, w2, w3):
            ref[0:2] = ref[TILE:slots]
        pot[:TILE] = pot[TILE:]
        rad[:TILE] = rad[TILE:]
        ready_high[...] = high[...]
        ready_low[...] = low[...]

        for i in range(TILE):
            own = s_in[i]
            before, at_low, at_high, after = slab_parts(own, near[i], far[i], s_)
            a0[i + 2, 0:TILE] = before
            a0[i + 2, TILE : 2 * TILE] = own[:TILE] + at_low
            if s_ > 2 * TILE:
                a0[i + 2, 2 * TILE : s_] = own[TILE : s_ - TILE]
            a0[i + 2, s_ : s_ + TILE] = own[s_ - TILE : s_] + at_high
            a0[i + 2, s_ + TILE : s_ + 2 * TILE] = after

        for n in range(1, ITERS + 1):
            past, weighted = levels_a[n - 1], levels_w[n - 1]
            columns = slice((n - 1) * share_ * r_, n * share_ * r_)
            one = jnp.dot(tab[...], ready_high[:, columns], preferred_element_type=jnp.float32)
            two = jnp.dot(tab[:out_rows], ready_low[:, columns], preferred_element_type=jnp.float32)
            solved = one[:out_rows] + one[out_rows:] + two
            for i in range(TILE):
                total = past[i] + past[i + 2] + rate[...] * past[i + 1]
                mid = weighted[i + 1]
                value = 6.0 * mid - (pltpu.roll(mid, 1, 0) + pltpu.roll(mid, rows - 1, 0)) + total
                if n < ITERS:
                    levels_a[n][i + 2] = total
                    levels_w[n][i + 2] = value
                else:
                    value = jnp.concatenate([value, jnp.zeros((held - rows, r_), jnp.float32)], 0)
                    top_part, rest_part = split(value)
                    high[:, i * r_ : (i + 1) * r_] = top_part
                    low[:, i * r_ : (i + 1) * r_] = rest_part
            solved = jnp.concatenate([solved[:, i * r_ : (i + 1) * r_] for i in range(share_)], 0)
            solved = jnp.dot(triple(solved), turn[...], preferred_element_type=jnp.float32)
            for i in range(share_):
                pot[TILE + (n - 1) * share_ + i] = solved[i * out_rows : (i + 1) * out_rows, :r_]
                rad[TILE + (n - 1) * share_ + i] = solved[i * out_rows : i * out_rows + s_, r_:]
            for i in range((n - 1) * share_, n * share_):
                at = LEAD - ORDER + 1 + i
                out = pl.ds(i, s_, stride=TILE)
                mid = pot[at]
                along = pltpu.roll(mid, out_rows - 1, 0) - pltpu.roll(mid, 1, 0)
                pressure[out, :] = mid[:s_]
                c0[out, :] = v0[out, :] - rad[at]
                c1[out, :] = v1[out, :] - 0.5 * (pot[at + 1, :s_] - pot[at - 1, :s_])
                c2[out, :] = v2[out, :] - 0.5 * along[:s_]

    def flat(ref):
        return ref.reshape(s_ * TILE, r_)

    def body(s_in, near, far, v, tab, turn, rate, corrected, pressure, *scratch):
        parts = [flat(v.at[i]) for i in range(3)]
        outs = [flat(corrected.at[i]) for i in range(3)]
        kernel(s_in, near, far, *parts, tab, turn, rate, *outs, flat(pressure), *scratch)

    at = lambda k: jnp.maximum(k - 3, 0)
    of = lambda k: jnp.minimum(k, steps - 1)
    slab = pltpu.VMEM((slots, rows, r_), jnp.float32)
    return pl.pallas_call(
        body,
        grid=(steps + 1,),
        in_specs=[
            pl.BlockSpec((TILE, s_ + TILE, r_), lambda k: (of(k), 0, 0)),
            pl.BlockSpec((TILE, TILE, r_), lambda k: (of(k), 0, 0)),
            pl.BlockSpec((TILE, TILE, r_), lambda k: (of(k), 0, 0)),
            pl.BlockSpec((3, s_, TILE, r_), lambda k: (0, 0, at(k), 0)),
            pl.BlockSpec((2 * out_rows, held), lambda k: (0, 0)),
            pl.BlockSpec((3 * r_, 2 * r_), lambda k: (0, 0)),
            pl.BlockSpec((1, r_), lambda k: (0, 0)),
        ],
        out_specs=[
            pl.BlockSpec((3, s_, TILE, r_), lambda k: (0, 0, at(k), 0)),
            pl.BlockSpec((s_, TILE, r_), lambda k: (0, at(k), 0)),
        ],
        out_shape=[
            jax.ShapeDtypeStruct(velocity.shape, jnp.float32),
            jax.ShapeDtypeStruct(velocity.shape[1:], jnp.float32),
        ],
        scratch_shapes=[slab] * 7
        + [pltpu.VMEM((held, TILE * r_), jnp.bfloat16)] * 4
        + [pltpu.VMEM((2 * TILE, out_rows, r_), jnp.float32), pltpu.VMEM((2 * TILE, s_, r_), jnp.float32)],
        compiler_params=pltpu.CompilerParams(vmem_limit_bytes=56 << 20),
        name="project",
    )(s_ext, pack_l, pack_r, velocity, table, back, rates)


def wall_call(s_ext, near_stations, near_walls, near_basis, stations):
    cells = s_ext.shape[1] - TILE
    table = wall_table(cells, wall_hops(cells))
    targets = near_stations.shape[0]
    if stations <= targets:
        return wall_part(s_ext, table, near_stations, near_walls, near_basis, stations)
    batch = max(d for d in range(TILE, 6 * TILE + 1, TILE) if targets % d == 0)
    index = jnp.arange(batch, dtype=jnp.int32)
    planes = [
        wall_part(s_ext, table[i : i + batch], index, near_walls, near_basis, batch) for i in range(0, targets, batch)
    ]
    select = (near_stations[:, None] == jnp.arange(stations)[None, :]).astype(jnp.float32)
    return jnp.dot(select.T, jnp.concatenate(planes, 0), precision=PRECISE)


def wall_part(s_ext, table, chosen, near_walls, near_basis, groups):
    wide, tall, r_ = s_ext.shape
    s_ = tall - TILE
    rows = tall + (-tall) % (2 * TILE)
    chunks = wide // TILE
    group = max(d for d in range(1, 4) if chunks % d == 0)
    steps = chunks // group
    targets = chosen.shape[0]
    pitch = rows + (-rows) % r_
    table = np.pad(table, ((0, 0), (0, 0), (0, pitch - tall))).reshape(targets, ORDER * pitch)
    top = table.astype(jnp.bfloat16)
    rest = (table - top.astype(np.float32)).astype(jnp.bfloat16)
    table = jnp.asarray(np.concatenate([top, rest], 0))
    modes = jnp.asarray(radial_modes(r_)[:WALL_SPAN].astype(np.float32))
    pick = (near_walls[:, None] == jnp.arange(WALL_SPAN)[None, :]).astype(jnp.float32)
    values = jnp.dot(pick, modes, precision=PRECISE)
    rates = jnp.asarray(radial_rates(r_))[None, :]
    tall_rows = ORDER * groups

    def kernel(s_in, tab, station, rate, value, base, out, parts, high, low, terms, old, new):
        k = pl.program_id(0)

        @pl.when(k == 0)
        def _():
            pick = (lax.broadcasted_iota(jnp.int32, (groups, targets), 0) == station[...]).astype(jnp.bfloat16)
            whole = jnp.dot(jnp.concatenate([pick, pick], axis=1), tab[...], preferred_element_type=jnp.float32)
            for j in range(ORDER):
                top, rest = split(whole[:, j * pitch : j * pitch + rows])
                parts[j * groups : (j + 1) * groups] = top
                parts[tall_rows + j * groups : tall_rows + (j + 1) * groups] = rest

        for c in range(group):
            for i in range(TILE):
                slab = s_in[c * TILE + i]
                if rows > tall:
                    slab = jnp.concatenate([slab, jnp.zeros((rows - tall, r_), jnp.float32)], 0)
                top, rest = split(slab)
                high[c, :, i * r_ : (i + 1) * r_] = top
                low[c, :, i * r_ : (i + 1) * r_] = rest
            one = jnp.dot(parts[...], high[c], preferred_element_type=jnp.float32)
            two = jnp.dot(parts[:tall_rows], low[c], preferred_element_type=jnp.float32)
            terms[k * group + c] = one[:tall_rows] + one[tall_rows:] + two

        @pl.when(k == steps - 1)
        def _():
            zero = jnp.zeros((groups, r_), jnp.float32)
            for ref in (old, new):
                ref[0] = zero
                ref[wide + 1] = zero
            first = (ORDER - 1) * groups

            def start(c, _):
                for i in range(TILE):
                    old[c * TILE + i + 1] = terms[c, first : first + groups, i * r_ : (i + 1) * r_]
                return 0

            lax.fori_loop(0, chunks, start, 0)
            source, target = old, new
            for j in range(ORDER - 2, -1, -1):

                def level(c, _, j=j, source=source, target=target):
                    for i in range(TILE):
                        t = c * TILE + i + 1
                        target[t] = (
                            source[t - 1]
                            + source[t + 1]
                            + rate[...] * source[t]
                            + terms[c, j * groups : (j + 1) * groups, i * r_ : (i + 1) * r_]
                        )
                    return 0

                lax.fori_loop(0, chunks, level, 0)
                source, target = target, source
            ones = jnp.ones((2 * r_, NA), jnp.bfloat16)

            def gather(c, total):
                at = [c * TILE + i for i in range(TILE)]
                product = jnp.concatenate([source[t + 1] * value[pl.ds(t, 1), :] for t in at], axis=0)
                top, rest = split(product)
                sums = jnp.dot(jnp.concatenate([top, rest], axis=1), ones, preferred_element_type=jnp.float32)
                for i, t in enumerate(at):
                    total = total + sums[i * groups : (i + 1) * groups] * base[pl.ds(t, 1), :]
                return total

            out[...] = lax.fori_loop(0, chunks, gather, jnp.zeros((groups, NA), jnp.float32))

    tile = pl.pallas_call(
        kernel,
        grid=(steps,),
        in_specs=[
            pl.BlockSpec((group * TILE, tall, r_), lambda k: (k, 0, 0)),
            pl.BlockSpec((2 * targets, ORDER * pitch), lambda k: (0, 0)),
            pl.BlockSpec((1, targets), lambda k: (0, 0)),
            pl.BlockSpec((1, r_), lambda k: (0, 0)),
            pl.BlockSpec((wide, r_), lambda k: (0, 0)),
            pl.BlockSpec((wide, NA), lambda k: (0, 0)),
        ],
        out_specs=pl.BlockSpec((groups, NA), lambda k: (0, 0)),
        out_shape=jax.ShapeDtypeStruct((groups, NA), jnp.float32),
        scratch_shapes=[
            pltpu.VMEM((2 * tall_rows, rows), jnp.bfloat16),
            pltpu.VMEM((group, rows, TILE * r_), jnp.bfloat16),
            pltpu.VMEM((group, rows, TILE * r_), jnp.bfloat16),
            pltpu.VMEM((chunks, tall_rows, TILE * r_), jnp.float32),
            pltpu.VMEM((wide + 2, groups, r_), jnp.float32),
            pltpu.VMEM((wide + 2, groups, r_), jnp.float32),
        ],
        compiler_params=pltpu.CompilerParams(vmem_limit_bytes=56 << 20),
        name="wall",
    )(s_ext, table, chosen[None, :], rates, values, near_basis)
    return tile


def azimuth_basis(first_cell, cells, total):
    column = jnp.arange(NA)
    upper = column >= NA // 2
    harmonic = jnp.where(upper, column - NA // 2 + 1, column)
    index = first_cell + jnp.arange(cells)
    phase = index[:, None] * harmonic[None, :] % total
    angle = 2.0 * math.pi / total * phase.astype(jnp.float32)
    return jnp.where(upper[None, :], jnp.sin(angle), jnp.cos(angle))


def bin_weights(scale):
    column = jnp.arange(NF)
    upper = column >= NF // 2
    harmonic = jnp.where(upper, column - NF // 2 + 1, column)
    phase = jnp.arange(NBIN)[:, None] * harmonic[None, :] % NBIN
    angle = 2.0 * math.pi / NBIN * phase.astype(jnp.float32)
    return jnp.where(upper[None, :], jnp.sin(angle), jnp.cos(angle)) * scale


def send(x, spans, planes, by_span, by_plane):
    pairs = []
    for i in range(spans):
        for j in range(planes):
            to = ((i + by_span) % spans) * planes + (j + by_plane) % planes
            pairs.append((i * planes + j, to))
    return lax.ppermute(x, ("span", "plane"), pairs)


def turn_exchange(s_ext, zr, zl, wall_index, spans, planes):
    theta_cells = wall_index.shape[0]
    tall = s_ext.shape[1]
    edge = ORDER + 1
    wide = s_ext.shape[0]
    first = LEAD - 1
    last = LEAD + theta_cells - ORDER
    after = LEAD - ORDER
    before = LEAD + theta_cells - 1

    def packed(at, walls):
        free = jnp.pad(walls.astype(jnp.float32), (0, zr.shape[2] - ORDER))
        own = zr[at : at + edge]
        own = jnp.where(jnp.arange(TILE)[None, :, None] == 1, free[None, None, :], own)
        return jnp.concatenate([s_ext[at : at + edge], own, zl[at : at + edge]], axis=1)

    low = send(packed(last, wall_index[-ORDER:]), spans, planes, 0, 1)
    high = send(packed(first, wall_index[:ORDER]), spans, planes, 0, -1)

    def unpacked():
        rows = jnp.arange(TILE)[None, :, None] != 1
        whole = []
        for mid, start in ((zr, tall), (zl, tall + TILE)):
            sides = []
            for piece, at in ((low, after), (high, before)):
                piece = piece[:, start : start + TILE]
                if start == tall:
                    piece = jnp.where(rows, piece, 0.0)
                sides.append(jnp.pad(piece, ((at, wide - at - edge), (0, 0), (0, 0))))
            whole.append(mid + sides[0] + sides[1])
        walls = [piece[0, tall + 1, :ORDER].astype(wall_index.dtype) for piece in (low, high)]
        none = jnp.full((wide,), -1, wall_index.dtype)
        walls = jnp.concatenate(
            [none[:after], walls[0], wall_index, walls[1], none[LEAD + theta_cells + ORDER :]], 0
        )
        return whole[0], whole[1], walls

    return low, high, unpacked


def span_exchange(zr, zl, spans, planes, span_cells):
    from_left = [send(zr, spans, planes, 1, 0)]
    from_right = [send(zl, spans, planes, -1, 0)]
    tables = []
    while len(from_left) < spans and np.any(hop_table(len(from_left) * span_cells)):
        table = hop_table(len(from_left) * span_cells)
        left_table = np.zeros((TILE, TILE), np.float32)
        left_table[: TILE - ORDER - 1 : -1, [0, 7, 6, 5, 4, 3]] = table
        right_table = np.zeros((TILE, TILE), np.float32)
        right_table[:ORDER, [7, 0, 1, 2, 3, 4]] = table
        tables.append((left_table, right_table))
        hop = len(from_left) + 1
        from_left.append(send(zr, spans, planes, hop, 0))
        from_right.append(send(zl, spans, planes, -hop, 0))
    return from_left, from_right, tables


def share(rows, spans, planes):
    each = rows.shape[0]
    here = lax.axis_index("plane")
    whole = jnp.zeros((planes,) + rows.shape, rows.dtype)
    order = jnp.arange(planes)[:, None, None]
    for step in range(planes):
        piece = rows if step == 0 else send(rows, spans, planes, 0, step)
        whole = jnp.where(order == (here - step) % planes, piece[None], whole)
    return whole.reshape(planes * each, rows.shape[1])


def local(velocity, wall_history, phase_bin, station_of, wall_index, spans, planes):
    _, span_cells, theta_cells, _ = velocity.shape
    total_theta = theta_cells * planes
    stations = ST_DEV * spans
    wide = theta_cells + 2 * TILE
    hops = wall_hops(span_cells)
    near_basis = azimuth_basis(lax.axis_index("plane") * theta_cells - LEAD, wide, total_theta)
    basis = near_basis[LEAD : LEAD + theta_cells]
    s_own, zr, zl = source_call(velocity)
    station_of, wall_index, s_own = lax.optimization_barrier((station_of, wall_index, s_own))
    low, high, unpacked = turn_exchange(s_own, zr, zl, wall_index, spans, planes)
    sides = [send(station_of, spans, planes, -h, 0) if h else station_of for h in range(-hops, hops + 1)]
    tiles = bins_call(wall_history, phase_bin, station_of, basis, stations)
    zr_wide, zl_wide, near_walls = unpacked()
    zr_wide, zl_wide, near_walls, sides, tiles = lax.optimization_barrier((zr_wide, zl_wide, near_walls, sides, tiles))
    from_left, from_right, tables = span_exchange(zr_wide, zl_wide, spans, planes, span_cells)
    near_stations = jnp.concatenate(sides, 0)
    wall = wall_call(s_own, near_stations, near_walls, near_basis, stations)
    newest = (jnp.arange(NBIN) == phase_bin[-1]).astype(jnp.float32)
    tiles = tiles + newest[None, :, None] * wall[:, None, :]
    from_left, from_right, tiles, s_own = lax.optimization_barrier((from_left, from_right, tiles, s_own))
    tall = span_cells + TILE
    s_ext = s_own.at[LEAD - ORDER : LEAD + 1].add(low[:, :tall])
    s_ext = s_ext.at[LEAD + theta_cells - 1 : LEAD + theta_cells + ORDER].add(high[:, :tall])
    pack_l, pack_r = from_left[0], from_right[0]
    for far_left, far_right, (left_table, right_table) in zip(from_left[1:], from_right[1:], tables):
        pack_l = pack_l + jnp.einsum("bd,adr->abr", left_table, far_left, precision=PRECISE)
        pack_r = pack_r + jnp.einsum("bd,adr->abr", right_table, far_right, precision=PRECISE)
    each = stations // (spans * planes)
    parts = lax.all_to_all(tiles, ("span", "plane"), split_axis=0, concat_axis=0, tiled=True)
    corrected, pressure = project_call(s_ext, pack_l, pack_r, velocity)
    parts, pressure = lax.optimization_barrier((parts, pressure))
    held = jnp.sum(parts.reshape(spans * planes, each, NBIN, NA), axis=0)
    weights = bin_weights(1.0 / math.sqrt(total_theta * (wall_history.shape[0] + 1)))
    mine = jnp.einsum("sba,bf->saf", held, weights, precision=PRECISE).reshape(each, NA * NF)
    coefficients = share(mine, spans, planes)
    return corrected, pressure, coefficients


def solution(mesh):
    spans = mesh.shape["span"]
    planes = mesh.shape["plane"]
    in_specs = (
        P(None, "span", "plane", None),
        P(None, "span", "plane"),
        P(),
        P("span"),
        P("plane"),
    )
    out_specs = (P(None, "span", "plane", None), P("span", "plane", None), P("span", None))

    def body(*args):
        return local(*args, spans, planes)

    return jax.shard_map(body, mesh=mesh, in_specs=in_specs, out_specs=out_specs, check_vma=False)
```
